256 devices in a mesh: seq: 32 (over x, z), head: 8 (over y, core).
Axes of the slice: x: 4, y: 4, z: 8, core: 2. Of those that a mesh axis runs over, the one named last changes fastest.
Arguments:
- queries: bfloat16 [16384, 16, 128], P('seq', 'head'), may hold values from -6 to 6
- keys: bfloat16 [16384, 16, 128], P('seq', 'head'), may hold values from -6 to 6
- values: bfloat16 [16384, 16, 256], P('seq', 'head'), may hold values from -15 to 15
- beta: float32 [16, 16384], P('head', 'seq'), may hold values from 0 to 0.9
- reset_blocks: int32 [32, 2], P('seq'), may hold values from 0 to 4, as said below
- out_weight: bfloat16 [4096, 4096], P('head'), may hold values from -0.09375 to 0.09375
Outputs:
- layer_out: bfloat16 [16384, 4096], P(('seq', 'head'))
The draws below stay inside these ranges and needn't reach their ends.
Inputs may be any that keep to these rules, and one draw needn't show every extreme that they name: `reset_blocks`: row s lists distinct local indices (0 to 3) of the blocks of sequence shard s at which an episode begins; unused slots hold 4.
All inputs are finite; a program needn't handle non-finite values.
Results may differ from the reference program's by a relative error of at most 0.017.
Values may be sent and summed in bfloat16 or wider, within the bound.
No kernel may reach another device: no remote copies, remote signals or barrier semaphores. Data moves between devices by JAX's collectives and lax.ppermute only.
A program may use at most 64 MiB of HBM per device.

```python
import math
import jax
import jax.numpy as jnp
from jax import lax

H = 16
DK = 128
DV = 256
D = 4096
BLOCK = 128
RESETS_MAX = 2
TOK_DEV = 512
TOKENS = 16384
BLOCKS_DEV = 4
SHARDS = 32
N_HEAD = 8


def draw_keys(key, part):
    streams = jax.random.split(key, 3)
    directions = jnp.clip(jax.random.normal(streams[0], (4, H, DK), jnp.float32), -4.0, 4.0)
    weights = jnp.clip(jax.random.normal(streams[1], (TOKENS, H, 4), jnp.float32), -3.0, 3.0)
    drawn = jnp.clip(jax.random.normal(streams[2], (TOKENS, H, DK), jnp.float32) * 0.58, -2.5, 2.5)
    for column in range(4):
        drawn = drawn + 0.5 * weights[:, :, column:column + 1] * directions[column][None, :, :]
    return jnp.clip(drawn, -6.0, 6.0).astype(jnp.bfloat16)


def draw_values(key, part):
    streams = jax.random.split(key, 2)
    scales = jnp.exp(jax.random.uniform(streams[0], (H, DV), jnp.float32) * math.log(10.0)) / 4.0
    noise = jnp.clip(jax.random.normal(streams[1], (TOKENS, H, DV), jnp.float32), -6.0, 6.0)
    drawn = noise * scales[None, :, :]
    return drawn.astype(jnp.bfloat16)


def draw_beta(key, part):
    streams = jax.random.split(key, 5)
    shuffled = jax.random.permutation(streams[0], H)
    position = jnp.argsort(shuffled)
    slow_count = H // 2
    fast_high = 0.3
    rough_low = 0.5
    rough_high = 1.5
    is_slow = position < slow_count
    slow_rate = DK / TOKENS * jnp.exp(jax.random.uniform(streams[1], (H,), jnp.float32, math.log(0.2), math.log(1.5)))
    fast_rate = jnp.exp(jax.random.uniform(streams[2], (H,), jnp.float32, math.log(0.05), math.log(fast_high)))
    head_rate = jnp.where(is_slow, slow_rate, fast_rate)
    shard_rate = jnp.exp(jax.random.uniform(streams[3], (TOKENS // TOK_DEV,), jnp.float32, math.log(0.5), math.log(2.0)))
    token_rate = jnp.repeat(shard_rate, TOK_DEV)
    roughness = jax.random.uniform(streams[4], (H, TOKENS), jnp.float32, rough_low, rough_high)
    return (head_rate[:, None] * token_rate[None, :] * roughness).astype(jnp.float32)


def draw_reset_blocks(key, part):
    streams = jax.random.split(key, 3)
    shard_keys = jax.random.split(streams[0], SHARDS)
    drawn_blocks = jax.vmap(lambda subkey: jax.random.permutation(subkey, BLOCKS_DEV))(shard_keys)[:, :RESETS_MAX]
    leading = (drawn_blocks[0] - drawn_blocks[0, 0]) % BLOCKS_DEV
    drawn_blocks = drawn_blocks.at[0].set(leading)
    target = jax.random.randint(streams[1], (), 1, SHARDS)
    target_fill = jax.random.randint(streams[2], (), 1, RESETS_MAX + 1)
    shard_ids = jnp.arange(SHARDS, dtype=jnp.int32)
    used = jnp.where(shard_ids == target, target_fill, 0).astype(jnp.int32)
    used = used.at[0].set(RESETS_MAX)
    slots = jnp.arange(RESETS_MAX, dtype=jnp.int32)
    filled = jnp.where(slots[None, :] < used[:, None], drawn_blocks, BLOCKS_DEV)
    return filled.astype(jnp.int32)


def block_levels(key, dims, cuts, least, largest):
    def one(dim, parts):
        draws = jax.random.uniform(jax.random.fold_in(jax.random.fold_in(key, 6), dim), (parts,), jnp.float32, least / len(cuts), largest / len(cuts))
        return jnp.repeat(jnp.exp(draws), dims[dim] // parts).reshape((-1,) + (1,) * (len(dims) - dim - 1))

    level = one(*cuts[0])
    for cut in cuts[1:]:
        level = level * one(*cut)
    return level


def normal_values(own_key, shape, scale, reach, shards=(), held_as=jnp.bfloat16):
    values = scale * jax.random.normal(own_key, shape, jnp.float32)
    if shards:
        values = values * block_levels(own_key, shape, shards, -0.22, 0.18)
    return jnp.clip(values, -reach, reach).astype(held_as)


def setup_inputs(seed: int = 0) -> dict:
    seeds = jax.random.split(jax.random.key(seed), 7)
    queries = normal_values(seeds[0], (TOKENS, H, DK), 1.0, 6.0, ((0, 32), (1, 8)))
    keys = draw_keys(jax.random.fold_in(seeds[6], 71), 0)
    values = draw_values(jax.random.fold_in(seeds[6], 71), 0)
    beta = draw_beta(jax.random.fold_in(seeds[6], 71), 0)
    reset_blocks = draw_reset_blocks(jax.random.fold_in(seeds[6], 71), 0)
    out_weight = normal_values(seeds[5], (H * DV, D), (H * DV) ** -0.5, 0.09375, ((0, 8),))
    return {"queries": queries, "keys": keys, "values": values, "beta": beta, "reset_blocks": reset_blocks, "out_weight": out_weight}


exact_precision = lax.Precision.HIGHEST

def unit_rows(values_in, epsilon):
    return values_in * lax.rsqrt(lax.optimization_barrier(jnp.sum(values_in * values_in, axis=-1, keepdims=True)) + epsilon)

def block_terms(query_rows, key_rows, value_rows, rate_rows):
    block_len = key_rows.shape[-2]
    key_dim = key_rows.shape[-1]
    strict = jnp.tril(jnp.ones((block_len, block_len), jnp.float32), -1)
    causal = jnp.tril(jnp.ones((block_len, block_len), jnp.float32))
    key_gram = jnp.einsum('...ik,...jk->...ij', key_rows, key_rows, precision=exact_precision)
    system = jnp.eye(block_len, dtype=jnp.float32) + rate_rows[..., :, None] * key_gram * strict
    right_side = rate_rows[..., :, None] * jnp.concatenate([key_rows, value_rows], axis=-1)
    solved = lax.linalg.triangular_solve(system, right_side, left_side=True, lower=True, unit_diagonal=True)
    attention_scores = jnp.einsum('...ik,...jk->...ij', query_rows, key_rows, precision=exact_precision) * causal
    return (solved[..., :key_dim], solved[..., key_dim:], attention_scores)

def reference(queries, keys, values, beta, reset_blocks, out_weight):
    tokens = queries.shape[0]
    block_count = tokens // BLOCK
    query_rows = unit_rows(queries.astype(jnp.float32), 1e-06).reshape(block_count, BLOCK, H, DK).transpose(0, 2, 1, 3)
    key_rows = unit_rows(keys.astype(jnp.float32), 1e-06).reshape(block_count, BLOCK, H, DK).transpose(0, 2, 1, 3)
    value_rows = values.astype(jnp.float32).reshape(block_count, BLOCK, H, DV).transpose(0, 2, 1, 3)
    rate_rows = beta.reshape(H, block_count, BLOCK).transpose(1, 0, 2)
    local_ids = jnp.arange(BLOCKS_DEV, dtype=jnp.int32)
    starts = jnp.any(reset_blocks[:, :, None] == local_ids[None, None, :], axis=1)
    retain = 1.0 - starts.reshape(block_count).astype(jnp.float32)

    def advance(memory_state, inputs):
        query_block_tile, key_block_tile, v_blk, r_blk, kept = inputs
        decay_rows, update_rows, attention_scores = block_terms(query_block_tile, key_block_tile, v_blk, r_blk)
        memory_state = memory_state * kept
        fresh_value_rows = update_rows - jnp.einsum('gzs,gso->gzo', decay_rows, memory_state, precision=exact_precision)
        output_matrix = jnp.einsum('gzs,gso->gzo', query_block_tile, memory_state, precision=exact_precision) + jnp.einsum('kra,kap->krp', attention_scores, fresh_value_rows, precision=exact_precision)
        memory_state = memory_state + jnp.einsum('glq,glr->gqr', key_block_tile, fresh_value_rows, precision=exact_precision)
        return (memory_state, output_matrix)
    initial = jnp.zeros((H, DK, DV), jnp.float32)
    _, attended = lax.scan(advance, initial, (query_rows, key_rows, value_rows, rate_rows, retain))
    scaled = attended * lax.rsqrt(lax.optimization_barrier(jnp.mean(attended * attended, axis=-1, keepdims=True)) + 1e-05)
    normed = scaled.astype(jnp.bfloat16).transpose(0, 2, 1, 3).reshape(tokens, H * DV)
    group_width = H * DV // N_HEAD
    summed = jnp.zeros((tokens, D), jnp.float32)
    for group_index in range(N_HEAD):
        lo_col = group_index * group_width
        part_sum = jnp.dot(normed[:, lo_col:lo_col + group_width].astype(jnp.float32), out_weight[lo_col:lo_col + group_width].astype(jnp.float32), preferred_element_type=jnp.float32).astype(jnp.bfloat16)
        summed = summed + lax.optimization_barrier(part_sum).astype(jnp.float32)
    return summed.astype(jnp.bfloat16)
```

```python
import jax
import jax.numpy as jnp
from jax import lax
from jax.experimental import pallas as pl
from jax.experimental.pallas import tpu as pltpu
from jax.sharding import PartitionSpec as P

BLOCK = 128
INTERPRET = False
VMEM_LIMIT = 48 << 20
F32 = jnp.float32
BF16 = jnp.bfloat16


def split(x):
    high = x.astype(BF16)
    return high, (x - high.astype(F32)).astype(BF16)


def dot(a, b):
    return jnp.dot(a, b, preferred_element_type=F32)


def dot_t(a, b):
    return lax.dot_general(a, b, (((0,), (0,)), ((), ())), preferred_element_type=F32)


def dot_nt(a, b):
    return lax.dot_general(a, b, (((1,), (1,)), ((), ())), preferred_element_type=F32)


def dot3(a, b):
    a_high, a_low = split(a)
    b_high, b_low = split(b)
    both = dot(jnp.concatenate([a_high, a_low], 1), jnp.concatenate([b_high, b_high], 0))
    return both + dot(a_high, b_low)


def dot2_right(a, b):
    b_high, b_low = split(b)
    return dot(jnp.concatenate([a, a], 1), jnp.concatenate([b_high, b_low], 0))


def dot2_left(a, b):
    a_high, a_low = split(a)
    return dot(jnp.concatenate([a_high, a_low], 1), jnp.concatenate([b, b], 0))


def square_ids(n):
    return lax.broadcasted_iota(jnp.int32, (n, n), 0), lax.broadcasted_iota(jnp.int32, (n, n), 1)


def terms_kernel(resets, k_ref, v_ref, beta_ref, wu_ref, prefix_ref, scale_ref, carry_ref):
    row, col = square_ids(BLOCK)
    eye = row == col
    identity = jnp.where(eye, 1.0, 0.0).astype(F32)
    cells = [(b, h) for b in range(4) for h in range(2)]
    ks, vs, grams = {}, {}, {}
    for b, h in cells:
        ks[b, h] = k_ref[b * BLOCK : (b + 1) * BLOCK, h * 128 : (h + 1) * 128]
        vs[b, h] = v_ref[b * BLOCK : (b + 1) * BLOCK, h * 256 : (h + 1) * 256]
        grams[b, h] = dot_nt(ks[b, h], ks[b, h])
    lower, inv, r_cols, beta_rows, c_rows = {}, {}, {}, {}, {}
    for b, h in cells:
        gram = grams[b, h]
        diagonal = jnp.where(eye, gram, 0.0)
        r_col = lax.rsqrt(jnp.sum(diagonal, axis=1, keepdims=True) + 1e-06)
        r_row = lax.rsqrt(jnp.sum(diagonal, axis=0, keepdims=True) + 1e-06)
        beta_row = beta_ref[h : h + 1, b * BLOCK : (b + 1) * BLOCK]
        beta_col = jnp.sum(jnp.where(eye, beta_row, 0.0), axis=1, keepdims=True)
        low = jnp.where(row > col, (beta_col * r_col) * gram * r_row, 0.0)
        lower[b, h] = low
        inv[b, h] = identity - jnp.where(row // 2 == col // 2, low, 0.0)
        r_cols[b, h] = r_col
        beta_rows[b, h] = beta_row
        c_rows[b, h] = beta_row * r_row
        scale_ref[b * 2 + h : b * 2 + h + 1, :] = r_row
    size = 2
    while size < BLOCK:
        joined = (row // (2 * size) == col // (2 * size)) & (row // size != col // size)
        half = {}
        for cell in cells:
            half[cell] = dot3(jnp.where(joined, lower[cell], 0.0), inv[cell])
        for cell in cells:
            inv[cell] = inv[cell] - dot3(inv[cell], half[cell])
        size *= 2
    steps = {}
    for b, h in cells:
        cell = (b, h)
        decay = dot2_left(inv[cell] * c_rows[cell], ks[cell])
        update = dot2_left(inv[cell] * beta_rows[cell], vs[cell])
        wu = jnp.concatenate([decay, update], 1)
        wu_ref[b * 2 + h] = wu
        high, low = split(wu * r_cols[cell])
        steps[cell] = dot_t(
            jnp.concatenate([ks[cell], ks[cell]], 0), jnp.concatenate([high, low], 0)
        )
    zeros = jnp.zeros((BLOCK, 256), F32)
    state = {h: jnp.concatenate([identity, zeros], 1) for h in range(2)}
    for b in range(4):
        starts = (resets[0] == b) | (resets[1] == b)
        kept = jnp.where(starts, 0.0, 1.0).astype(F32)
        for h in range(2):
            before = state[h] * kept
            prefix_ref[b * 2 + h] = before
            step = steps[b, h]
            added = jnp.concatenate([jnp.zeros((BLOCK, 128), F32), step[:, 128:]], 1)
            if b == 0:
                moved = jnp.concatenate([step[:, :128] * kept, zeros], 1)
            else:
                moved = dot3(step[:, :128], before)
            state[h] = before - moved + added
    for h in range(2):
        carry_ref[h] = jnp.concatenate(
            [state[h][:, :128] - identity, state[h][:, 128:]], 1
        ).astype(BF16)


def response_kernel(q_ref, k_ref, scale_ref, wu_ref, prefix_ref, r_ref, o_ref):
    row, col = square_ids(BLOCK)
    causal = row >= col
    for b in range(4):
        for h in range(2):
            cell = b * 2 + h
            q = q_ref[b * BLOCK : (b + 1) * BLOCK, h * 128 : (h + 1) * 128]
            k = k_ref[b * BLOCK : (b + 1) * BLOCK, h * 128 : (h + 1) * 128]
            qf = q.astype(F32)
            rq = lax.rsqrt(jnp.sum(qf * qf, axis=1, keepdims=True) + 1e-06)
            scores = jnp.where(causal, rq * dot_nt(q, k) * scale_ref[cell : cell + 1, :], 0.0)
            local = dot3(scores, wu_ref[cell])
            reach = qf * rq - local[:, :128]
            out = dot3(reach, prefix_ref[cell])
            r_ref[cell] = out[:, :128].astype(BF16)
            o_ref[cell] = out[:, 128:] + local[:, 128:]


def follow(state, element):
    moved = dot2_right(element[:, :128], state)
    width = state.shape[1]
    added = element.astype(F32)
    if width == 256:
        added = added[:, 128:]
    else:
        added = jnp.concatenate([jnp.zeros((BLOCK, 128), F32), added[:, 128:]], 1)
    return state + moved + added


def group_kernel(place, *refs):
    elements, (before_ref, total_ref) = refs[:8], refs[8:]
    row, col = square_ids(BLOCK)
    identity = jnp.where(row == col, 1.0, 0.0).astype(F32)
    empty = jnp.concatenate([identity, jnp.zeros((BLOCK, 256), F32)], 1)
    z = place[0]
    state = {h: empty for h in range(2)}
    after = {h: empty for h in range(2)}
    for step in range(1, 8):
        wraps = z + step == 8
        for h in range(2):
            if step > 1:
                after[h] = jnp.where(wraps, state[h], after[h])
                state[h] = jnp.where(wraps, empty, state[h])
            state[h] = follow(state[h], elements[step][h])
    for h in range(2):
        after[h] = jnp.where(z == 0, state[h], after[h])
        state[h] = jnp.where(z == 0, empty, state[h])
        before_ref[h] = jnp.concatenate([state[h][:, :128] - identity, state[h][:, 128:]], 1)
        through = follow(state[h], elements[0][h])
        total = dot3(after[h][:, :128], through)
        total_ref[h] = jnp.concatenate(
            [total[:, :128] - identity, total[:, 128:] + after[h][:, 128:]], 1
        ).astype(BF16)


def output_kernel(place, far_ref, mid_ref, near_ref, before_ref, r_ref, o_ref, keep_ref, send_ref):
    y, core = place[1], place[2]
    states = []
    for h in range(2):
        state = far_ref[h][:, 128:].astype(F32)
        state = follow(state, mid_ref[h])
        state = follow(state, near_ref[h])
        before = before_ref[h]
        states.append(state + dot3(before[:, :128], state) + before[:, 128:])
    for b in range(4):
        parts = []
        for h in range(2):
            cell = b * 2 + h
            out = dot2_right(r_ref[cell], states[h]) + o_ref[cell]
            mean = jnp.mean(out * out, axis=1, keepdims=True)
            parts.append((out * lax.rsqrt(mean + 1e-05)).astype(BF16))
        normed = jnp.concatenate(parts, 1)
        first, second = normed[:64], normed[64:]
        slot = pl.multiple_of(((4 - (y ^ b)) & 3) * 64, 64)
        keep_ref[pl.ds(slot, 64), :] = jnp.where(core == 0, first, second)
        send_ref[pl.ds(slot, 64), :] = jnp.where(core == 0, second, first)


SMEM = pl.BlockSpec(memory_space=pltpu.SMEM)
VMEM = pl.BlockSpec(memory_space=pltpu.VMEM)


def call(kernel, outs, scalars, arrays, flops):
    moved = sum(a.size * a.dtype.itemsize for a in list(arrays) + list(outs))
    return pl.pallas_call(
        kernel,
        out_shape=outs,
        in_specs=[SMEM] + [VMEM] * len(arrays) if scalars is not None else [VMEM] * len(arrays),
        out_specs=[VMEM] * len(outs),
        compiler_params=pltpu.CompilerParams(vmem_limit_bytes=VMEM_LIMIT),
        cost_estimate=pl.CostEstimate(flops=flops, bytes_accessed=moved, transcendentals=0),
        interpret=INTERPRET,
    )(*([scalars] if scalars is not None else []), *arrays)


def body(queries, keys, values, beta, reset_blocks, out_weight):
    q = queries.reshape(512, 256)
    k = keys.reshape(512, 256)
    v = values.reshape(512, 512)
    shard = lax.axis_index("seq")
    head = lax.axis_index("head")
    place = jnp.stack([shard % 8, head // 2, head % 2]).astype(jnp.int32)

    across = [(i, i ^ 1) for i in range(8)]
    other_weight = lax.ppermute(out_weight, "head", across)

    shaped = jax.ShapeDtypeStruct
    wu, prefix, scale, carry = call(
        terms_kernel,
        [
            shaped((8, 128, 384), F32),
            shaped((8, 128, 384), F32),
            shaped((8, 128), F32),
            shaped((2, 128, 384), BF16),
        ],
        reset_blocks.reshape(2),
        [k, v, beta],
        3_000_000_000,
    )
    up = [(i, i - i % 8 + (i + 1) % 8) for i in range(32)]
    down = [(i, i - i % 8 + (i + 7) % 8) for i in range(32)]
    below, above = [carry], [carry]
    for step in range(4):
        below.append(lax.ppermute(below[-1], "seq", up))
        if step < 3:
            above.append(lax.ppermute(above[-1], "seq", down))
    response, own_out = call(
        response_kernel,
        [shaped((8, 128, 128), BF16), shaped((8, 128, 256), F32)],
        None,
        [q, k, scale, wu, prefix],
        2_000_000_000,
    )
    before, total = call(
        group_kernel,
        [shaped((2, 128, 384), F32), shaped((2, 128, 384), BF16)],
        place,
        above + below[:0:-1],
        1_000_000_000,
    )
    received = [
        lax.ppermute(total, "seq", [(i, i + 8 * d) for i in range(32) if i + 8 * d < 32])
        for d in (3, 2, 1)
    ]
    keep, send = call(
        output_kernel,
        [shaped((256, 512), BF16), shaped((256, 512), BF16)],
        place,
        received + [before, response, own_out],
        500_000_000,
    )
    joined = lax.ppermute(send, "head", across)

    def product(first, last, low, high):
        return (
            dot(keep[first:last], out_weight[:, low:high])
            + dot(joined[first:last], other_weight[:, low:high])
        ).astype(BF16)

    near = [(i, i ^ 2) for i in range(8)]
    far = [(i, 7 - i ^ 1) for i in range(8)]
    sent_a = lax.ppermute(product(128, 256, 0, 2048), "head", near)
    sent_b = lax.ppermute(product(64, 192, 2048, 4096), "head", far)
    own_a = product(0, 128, 0, 2048)
    own_b0 = product(0, 64, 2048, 4096)
    own_b3 = product(192, 256, 2048, 4096)

    def add(x, y):
        return x.astype(F32) + y.astype(F32)

    next_a = lax.ppermute(add(own_a[64:], sent_a[:64]).astype(BF16), "head", far)
    next_b = lax.ppermute(add(own_b3, sent_b[64:]).astype(BF16), "head", near)
    out_a = (add(own_a[:64], sent_a[64:]) + next_a.astype(F32)).astype(BF16)
    out_b = (add(own_b0, sent_b[:64]) + next_b.astype(F32)).astype(BF16)
    return jnp.concatenate([out_a, out_b], 1)


def solution(mesh):
    return jax.shard_map(
        body,
        mesh=mesh,
        in_specs=(
            P("seq", "head", None),
            P("seq", "head", None),
            P("seq", "head", None),
            P("head", "seq"),
            P("seq", None),
            P("head", None),
        ),
        out_specs=P(("seq", "head"), None),
        check_vma=False,
    )
```

```python
import functools

import jax
import jax.numpy as jnp
from jax import lax
from jax.experimental import pallas as pl
from jax.experimental.pallas import tpu as pltpu
from jax.sharding import PartitionSpec as P

BLOCK = 128
INTERPRET = False
VMEM_LIMIT = 12 << 20
F32 = jnp.float32
BF16 = jnp.bfloat16


def split(x):
    high = x.astype(BF16)
    return high, (x - high.astype(F32)).astype(BF16)


def dot(a, b):
    return jnp.dot(a, b, preferred_element_type=F32)


def dot_t(a, b):
    return lax.dot_general(a, b, (((0,), (0,)), ((), ())), preferred_element_type=F32)


def dot_nt(a, b):
    return lax.dot_general(a, b, (((1,), (1,)), ((), ())), preferred_element_type=F32)


def dot3(a, b):
    a_high, a_low = split(a)
    b_high, b_low = split(b)
    both = dot(jnp.concatenate([a_high, a_low], 1), jnp.concatenate([b_high, b_high], 0))
    return both + dot(a_high, b_low)


def dot2_right(a, b):
    b_high, b_low = split(b)
    return dot(jnp.concatenate([a, a], 1), jnp.concatenate([b_high, b_low], 0))


def dot2_left(a, b):
    a_high, a_low = split(a)
    return dot(jnp.concatenate([a_high, a_low], 1), jnp.concatenate([b, b], 0))


def square_ids(n):
    return lax.broadcasted_iota(jnp.int32, (n, n), 0), lax.broadcasted_iota(jnp.int32, (n, n), 1)


def terms_kernel(resets, k_ref, v_ref, beta_ref, wu_ref, prefix_ref, scale_ref, carry_ref):
    row, col = square_ids(BLOCK)
    eye = row == col
    identity = jnp.where(eye, 1.0, 0.0).astype(F32)
    cells = [(b, h) for b in range(4) for h in range(2)]
    ks, vs, grams = {}, {}, {}
    for b, h in cells:
        ks[b, h] = k_ref[b * BLOCK : (b + 1) * BLOCK, h * 128 : (h + 1) * 128]
        vs[b, h] = v_ref[b * BLOCK : (b + 1) * BLOCK, h * 256 : (h + 1) * 256]
        grams[b, h] = dot_nt(ks[b, h], ks[b, h])
    lower, inv, r_cols, beta_rows, c_rows = {}, {}, {}, {}, {}
    for b, h in cells:
        gram = grams[b, h]
        diagonal = jnp.where(eye, gram, 0.0)
        r_col = lax.rsqrt(jnp.sum(diagonal, axis=1, keepdims=True) + 1e-06)
        r_row = lax.rsqrt(jnp.sum(diagonal, axis=0, keepdims=True) + 1e-06)
        beta_row = beta_ref[h : h + 1, b * BLOCK : (b + 1) * BLOCK]
        beta_col = jnp.sum(jnp.where(eye, beta_row, 0.0), axis=1, keepdims=True)
        low = jnp.where(row > col, (beta_col * r_col) * gram * r_row, 0.0)
        lower[b, h] = low
        inv[b, h] = identity - jnp.where(row // 2 == col // 2, low, 0.0)
        r_cols[b, h] = r_col
        beta_rows[b, h] = beta_row
        c_rows[b, h] = beta_row * r_row
        scale_ref[b * 2 + h : b * 2 + h + 1, :] = r_row
    size = 2
    while size < BLOCK:
        joined = (row // (2 * size) == col // (2 * size)) & (row // size != col // size)
        half = {}
        for cell in cells:
            half[cell] = dot3(jnp.where(joined, lower[cell], 0.0), inv[cell])
        for cell in cells:
            inv[cell] = inv[cell] - dot3(inv[cell], half[cell])
        size *= 2
    steps = {}
    for b, h in cells:
        cell = (b, h)
        decay = dot2_left(inv[cell] * c_rows[cell], ks[cell])
        update = dot2_left(inv[cell] * beta_rows[cell], vs[cell])
        wu = jnp.concatenate([decay, update], 1)
        wu_ref[b * 2 + h] = wu
        high, low = split(wu * r_cols[cell])
        steps[cell] = dot_t(
            jnp.concatenate([ks[cell], ks[cell]], 0), jnp.concatenate([high, low], 0)
        )
    zeros = jnp.zeros((BLOCK, 256), F32)
    state = {h: jnp.concatenate([identity, zeros], 1) for h in range(2)}
    for b in range(4):
        starts = (resets[0] == b) | (resets[1] == b)
        kept = jnp.where(starts, 0.0, 1.0).astype(F32)
        for h in range(2):
            before = state[h] * kept
            prefix_ref[b * 2 + h] = before
            step = steps[b, h]
            added = jnp.concatenate([jnp.zeros((BLOCK, 128), F32), step[:, 128:]], 1)
            if b == 0:
                moved = jnp.concatenate([step[:, :128] * kept, zeros], 1)
            else:
                moved = dot3(step[:, :128], before)
            state[h] = before - moved + added
    for h in range(2):
        carry_ref[h] = jnp.concatenate(
            [state[h][:, :128] - identity, state[h][:, 128:]], 1
        ).astype(BF16)


def response_kernel(q_ref, k_ref, scale_ref, wu_ref, prefix_ref, r_ref, o_ref):
    row, col = square_ids(BLOCK)
    causal = row >= col
    for b in range(4):
        for h in range(2):
            cell = b * 2 + h
            q = q_ref[b * BLOCK : (b + 1) * BLOCK, h * 128 : (h + 1) * 128]
            k = k_ref[b * BLOCK : (b + 1) * BLOCK, h * 128 : (h + 1) * 128]
            qf = q.astype(F32)
            rq = lax.rsqrt(jnp.sum(qf * qf, axis=1, keepdims=True) + 1e-06)
            scores = jnp.where(causal, rq * dot_nt(q, k) * scale_ref[cell : cell + 1, :], 0.0)
            local = dot3(scores, wu_ref[cell])
            reach = qf * rq - local[:, :128]
            out = dot3(reach, prefix_ref[cell])
            r_ref[cell] = out[:, :128].astype(BF16)
            o_ref[cell] = out[:, 128:] + local[:, 128:]


def follow(state, element):
    moved = dot2_right(element[:, :128], state)
    width = state.shape[1]
    added = element.astype(F32)
    if width == 256:
        added = added[:, 128:]
    else:
        added = jnp.concatenate([jnp.zeros((BLOCK, 128), F32), added[:, 128:]], 1)
    return state + moved + added


def group_kernel(*refs):
    elements, (before_ref, total_ref) = refs[:8], refs[8:]
    row, col = square_ids(BLOCK)
    identity = jnp.where(row == col, 1.0, 0.0).astype(F32)
    empty = jnp.concatenate([identity, jnp.zeros((BLOCK, 256), F32)], 1)
    z = lax.axis_index("seq") % 8
    state = {h: empty for h in range(2)}
    after = {h: empty for h in range(2)}
    for step in range(1, 8):
        wraps = z + step == 8
        for h in range(2):
            if step > 1:
                after[h] = jnp.where(wraps, state[h], after[h])
                state[h] = jnp.where(wraps, empty, state[h])
            state[h] = follow(state[h], elements[step][h])
    for h in range(2):
        after[h] = jnp.where(z == 0, state[h], after[h])
        state[h] = jnp.where(z == 0, empty, state[h])
        before_ref[h] = jnp.concatenate([state[h][:, :128] - identity, state[h][:, 128:]], 1)
        through = follow(state[h], elements[0][h])
        total = dot3(after[h][:, :128], through)
        total_ref[h] = jnp.concatenate(
            [total[:, :128] - identity, total[:, 128:] + after[h][:, 128:]], 1
        ).astype(BF16)


def output_kernel(far_ref, mid_ref, near_ref, before_ref, r_ref, o_ref, keep_ref, send_ref):
    head = lax.axis_index("head")
    y, core = head // 2, head % 2
    states = []
    for h in range(2):
        state = far_ref[h][:, 128:].astype(F32)
        state = follow(state, mid_ref[h])
        state = follow(state, near_ref[h])
        before = before_ref[h]
        states.append(state + dot3(before[:, :128], state) + before[:, 128:])
    for b in range(4):
        parts = []
        for h in range(2):
            cell = b * 2 + h
            out = dot2_right(r_ref[cell], states[h]) + o_ref[cell]
            mean = jnp.mean(out * out, axis=1, keepdims=True)
            parts.append((out * lax.rsqrt(mean + 1e-05)).astype(BF16))
        normed = jnp.concatenate(parts, 1)
        first, second = normed[:64], normed[64:]
        slot = pl.multiple_of(((4 - (y ^ b)) & 3) * 64, 64)
        keep_ref[pl.ds(slot, 64), :] = jnp.where(core == 0, first, second)
        send_ref[pl.ds(slot, 64), :] = jnp.where(core == 0, second, first)


SMEM = pl.BlockSpec(memory_space=pltpu.SMEM)
VMEM = pl.BlockSpec(memory_space=pltpu.VMEM)


def call(kernel, outs, scalars, arrays, flops):
    moved = sum(a.size * a.dtype.itemsize for a in list(arrays) + list(outs))
    return pl.pallas_call(
        kernel,
        out_shape=outs,
        in_specs=[SMEM] + [VMEM] * len(arrays) if scalars is not None else [VMEM] * len(arrays),
        out_specs=[VMEM] * len(outs),
        compiler_params=pltpu.CompilerParams(vmem_limit_bytes=VMEM_LIMIT),
        cost_estimate=pl.CostEstimate(flops=flops, bytes_accessed=moved, transcendentals=0),
        interpret=INTERPRET,
    )(*([scalars] if scalars is not None else []), *arrays)


def product_kernel(crossed, keep_ref, joined_ref, own_w_ref, other_w_ref, send_ref, own_ref):
    out = dot(keep_ref[...], own_w_ref[...]) + dot(joined_ref[...], other_w_ref[...])
    out = out.astype(BF16)
    if crossed:
        send_ref[...] = out[64:192]
        own_ref[:64] = out[:64]
        own_ref[64:] = out[192:]
    else:
        send_ref[...] = out[128:]
        own_ref[...] = out[:128]


def product(crossed, keep, joined, own_weight, other_weight):
    tile = 512
    first = 2048 // tile if crossed else 0
    rows = pl.BlockSpec((256, 512), lambda i: (0, 0))
    columns = pl.BlockSpec((512, tile), lambda i: (0, i + first))
    out = pl.BlockSpec((128, tile), lambda i: (0, i))
    return pl.pallas_call(
        functools.partial(product_kernel, crossed),
        grid=(2048 // tile,),
        out_shape=[jax.ShapeDtypeStruct((128, 2048), BF16)] * 2,
        in_specs=[rows, rows, columns, columns],
        out_specs=[out, out],
        compiler_params=pltpu.CompilerParams(vmem_limit_bytes=VMEM_LIMIT),
        cost_estimate=pl.CostEstimate(
            flops=1_000_000_000, bytes_accessed=6_000_000, transcendentals=0
        ),
        interpret=INTERPRET,
    )(keep, joined, own_weight, other_weight)


def body(queries, keys, values, beta, reset_blocks, out_weight):
    q = queries.reshape(512, 256)
    k = keys.reshape(512, 256)
    v = values.reshape(512, 512)
    across = [(i, i ^ 1) for i in range(8)]
    other_weight = lax.ppermute(out_weight, "head", across)

    shaped = jax.ShapeDtypeStruct
    wu, prefix, scale, carry = call(
        terms_kernel,
        [
            shaped((8, 128, 384), F32),
            shaped((8, 128, 384), F32),
            shaped((8, 128), F32),
            shaped((2, 128, 384), BF16),
        ],
        reset_blocks.reshape(2),
        [k, v, beta],
        3_000_000_000,
    )
    response, own_out = call(
        response_kernel,
        [shaped((8, 128, 128), BF16), shaped((8, 128, 256), F32)],
        None,
        [q, k, scale, wu, prefix],
        2_000_000_000,
    )
    up = [(i, i - i % 8 + (i + 1) % 8) for i in range(32)]
    down = [(i, i - i % 8 + (i + 7) % 8) for i in range(32)]
    below, above = [carry], [carry]
    for step in range(4):
        lower = lax.ppermute(below[-1], "seq", up)
        below.append(lower)
        if step < 3:
            above.append(lax.ppermute(above[-1], "seq", down))
        if step == 0:
            below[1], above[1], response, own_out = lax.optimization_barrier(
                (below[1], above[1], response, own_out)
            )
    before, total = call(
        group_kernel,
        [shaped((2, 128, 384), F32), shaped((2, 128, 384), BF16)],
        None,
        above + below[:0:-1],
        1_000_000_000,
    )
    received = [
        lax.ppermute(total, "seq", [(i, i + 8 * d) for i in range(32) if i + 8 * d < 32])
        for d in (3, 2, 1)
    ]
    keep, send = call(
        output_kernel,
        [shaped((256, 512), BF16), shaped((256, 512), BF16)],
        None,
        received + [before, response, own_out],
        500_000_000,
    )
    joined = lax.ppermute(send, "head", across)

    near = [(i, i ^ 2) for i in range(8)]
    far = [(i, i ^ 6) for i in range(8)]
    send_a, own_a = product(False, keep, joined, out_weight, other_weight)
    sent_a = lax.ppermute(send_a, "head", near)
    send_b, own_b = product(True, keep, joined, out_weight, other_weight)
    sent_b = lax.ppermute(send_b, "head", far)

    def add(x, y):
        return x.astype(F32) + y.astype(F32)

    next_a = lax.ppermute(add(own_a[64:], sent_a[:64]).astype(BF16), "head", far)
    next_b = lax.ppermute(add(own_b[64:], sent_b[64:]).astype(BF16), "head", near)
    out_a = (add(own_a[:64], sent_a[64:]) + next_a.astype(F32)).astype(BF16)
    out_b = (add(own_b[:64], sent_b[:64]) + next_b.astype(F32)).astype(BF16)
    return jnp.concatenate([out_a, out_b], 1)


def solution(mesh):
    return jax.shard_map(
        body,
        mesh=mesh,
        in_specs=(
            P("seq", "head", None),
            P("seq", "head", None),
            P("seq", "head", None),
            P("head", "seq"),
            P("seq", None),
            P("head", None),
        ),
        out_specs=P(("seq", "head"), None),
        check_vma=False,
    )
```

```python
import functools

import jax
import jax.numpy as jnp
from jax import lax
from jax.experimental import pallas as pl
from jax.experimental.pallas import tpu as pltpu
from jax.sharding import PartitionSpec as P

BLOCK = 128
INTERPRET = False
VMEM_LIMIT = 12 << 20
CHUNK = 1024
F32 = jnp.float32
BF16 = jnp.bfloat16


def split(x):
    high = x.astype(BF16)
    return high, (x - high.astype(F32)).astype(BF16)


def dot(a, b):
    return jnp.dot(a, b, preferred_element_type=F32)


def dot_t(a, b):
    return lax.dot_general(a, b, (((0,), (0,)), ((), ())), preferred_element_type=F32)


def dot_nt(a, b):
    return lax.dot_general(a, b, (((1,), (1,)), ((), ())), preferred_element_type=F32)


def dot3(a, b):
    a_high, a_low = split(a)
    b_high, b_low = split(b)
    both = dot(jnp.concatenate([a_high, a_low], 1), jnp.concatenate([b_high, b_high], 0))
    return both + dot(a_high, b_low)


def dot2_right(a, b):
    b_high, b_low = split(b)
    return dot(jnp.concatenate([a, a], 1), jnp.concatenate([b_high, b_low], 0))


def dot2_left(a, b):
    a_high, a_low = split(a)
    return dot(jnp.concatenate([a_high, a_low], 1), jnp.concatenate([b, b], 0))


def square_ids(n):
    return lax.broadcasted_iota(jnp.int32, (n, n), 0), lax.broadcasted_iota(jnp.int32, (n, n), 1)


def terms_kernel(
    resets_hbm, beta_hbm, k_ref, v_ref, wu_ref, prefix_ref, scale_ref, carry_ref, resets, beta_ref, sems
):
    resets_copy = pltpu.make_async_copy(resets_hbm, resets, sems.at[0])
    beta_copy = pltpu.make_async_copy(beta_hbm, beta_ref, sems.at[1])
    beta_copy.start()
    resets_copy.start()
    row, col = square_ids(BLOCK)
    eye = row == col
    identity = jnp.where(eye, 1.0, 0.0).astype(F32)
    cells = [(b, h) for b in range(4) for h in range(2)]
    ks, vs, grams = {}, {}, {}
    for b, h in cells:
        ks[b, h] = k_ref[b * BLOCK : (b + 1) * BLOCK, h * 128 : (h + 1) * 128]
        vs[b, h] = v_ref[b * BLOCK : (b + 1) * BLOCK, h * 256 : (h + 1) * 256]
        grams[b, h] = dot_nt(ks[b, h], ks[b, h])
    beta_copy.wait()
    lower, inv, r_cols, beta_rows, c_rows = {}, {}, {}, {}, {}
    for b, h in cells:
        gram = grams[b, h]
        diagonal = jnp.where(eye, gram, 0.0)
        r_col = lax.rsqrt(jnp.sum(diagonal, axis=1, keepdims=True) + 1e-06)
        r_row = lax.rsqrt(jnp.sum(diagonal, axis=0, keepdims=True) + 1e-06)
        beta_row = beta_ref[h : h + 1, b * BLOCK : (b + 1) * BLOCK]
        beta_col = jnp.sum(jnp.where(eye, beta_row, 0.0), axis=1, keepdims=True)
        low = jnp.where(row > col, (beta_col * r_col) * gram * r_row, 0.0)
        lower[b, h] = low
        inv[b, h] = identity - jnp.where(row // 2 == col // 2, low, 0.0)
        r_cols[b, h] = r_col
        beta_rows[b, h] = beta_row
        c_rows[b, h] = beta_row * r_row
        scale_ref[b * 2 + h : b * 2 + h + 1, :] = r_row
    size = 2
    while size < BLOCK:
        joined = (row // (2 * size) == col // (2 * size)) & (row // size != col // size)
        half = {}
        for cell in cells:
            half[cell] = dot3(jnp.where(joined, lower[cell], 0.0), inv[cell])
        for cell in cells:
            inv[cell] = inv[cell] - dot3(inv[cell], half[cell])
        size *= 2
    steps = {}
    for b, h in cells:
        cell = (b, h)
        decay = dot2_left(inv[cell] * c_rows[cell], ks[cell])
        update = dot2_left(inv[cell] * beta_rows[cell], vs[cell])
        wu = jnp.concatenate([decay, update], 1)
        wu_ref[b * 2 + h] = wu
        high, low = split(wu * r_cols[cell])
        steps[cell] = dot_t(
            jnp.concatenate([ks[cell], ks[cell]], 0), jnp.concatenate([high, low], 0)
        )
    zeros = jnp.zeros((BLOCK, 256), F32)
    state = {h: jnp.concatenate([identity, zeros], 1) for h in range(2)}
    resets_copy.wait()
    for b in range(4):
        starts = (resets[0, 0] == b) | (resets[0, 1] == b)
        kept = jnp.where(starts, 0.0, 1.0).astype(F32)
        for h in range(2):
            before = state[h] * kept
            prefix_ref[b * 2 + h] = before
            step = steps[b, h]
            added = jnp.concatenate([jnp.zeros((BLOCK, 128), F32), step[:, 128:]], 1)
            if b == 0:
                moved = jnp.concatenate([step[:, :128] * kept, zeros], 1)
            else:
                moved = dot3(step[:, :128], before)
            state[h] = before - moved + added
    for h in range(2):
        carry_ref[h] = jnp.concatenate(
            [state[h][:, :128] - identity, state[h][:, 128:]], 1
        ).astype(BF16)


def response_kernel(q_ref, k_ref, scale_ref, wu_ref, prefix_ref, r_ref, o_ref):
    row, col = square_ids(BLOCK)
    causal = row >= col
    for b in range(4):
        for h in range(2):
            cell = b * 2 + h
            q = q_ref[b * BLOCK : (b + 1) * BLOCK, h * 128 : (h + 1) * 128]
            k = k_ref[b * BLOCK : (b + 1) * BLOCK, h * 128 : (h + 1) * 128]
            qf = q.astype(F32)
            rq = lax.rsqrt(jnp.sum(qf * qf, axis=1, keepdims=True) + 1e-06)
            scores = jnp.where(causal, rq * dot_nt(q, k) * scale_ref[cell : cell + 1, :], 0.0)
            local = dot3(scores, wu_ref[cell])
            reach = qf * rq - local[:, :128]
            out = dot3(reach, prefix_ref[cell])
            r_ref[cell] = out[:, :128].astype(BF16)
            o_ref[cell] = out[:, 128:] + local[:, 128:]


def follow(state, element):
    moved = dot2_right(element[:, :128], state)
    width = state.shape[1]
    added = element.astype(F32)
    if width == 256:
        added = added[:, 128:]
    else:
        added = jnp.concatenate([jnp.zeros((BLOCK, 128), F32), added[:, 128:]], 1)
    return state + moved + added


def group_kernel(*refs):
    refs, (before_ref, total_ref) = refs[:9], refs[9:]
    elements = [(ref.at[0], ref.at[1]) for ref in refs[:4] + refs[6:]]
    elements.insert(4, refs[4:6])
    row, col = square_ids(BLOCK)
    identity = jnp.where(row == col, 1.0, 0.0).astype(F32)
    empty = jnp.concatenate([identity, jnp.zeros((BLOCK, 256), F32)], 1)
    z = lax.axis_index("seq") % 8
    state = {h: empty for h in range(2)}
    after = {h: empty for h in range(2)}
    for step in range(1, 8):
        wraps = z + step == 8
        for h in range(2):
            if step > 1:
                after[h] = jnp.where(wraps, state[h], after[h])
                state[h] = jnp.where(wraps, empty, state[h])
            state[h] = follow(state[h], elements[step][h][...])
    for h in range(2):
        after[h] = jnp.where(z == 0, state[h], after[h])
        state[h] = jnp.where(z == 0, empty, state[h])
        before_ref[h] = jnp.concatenate([state[h][:, :128] - identity, state[h][:, 128:]], 1)
        through = follow(state[h], elements[0][h][...])
        total = dot3(after[h][:, :128], through)
        total_ref[h] = jnp.concatenate(
            [total[:, :128] - identity, total[:, 128:] + after[h][:, 128:]], 1
        ).astype(BF16)


def output_kernel(far_ref, mid_ref, near_ref, before_ref, r_ref, o_ref, keep_ref, send_ref):
    head = lax.axis_index("head")
    y, core = head // 2, head % 2
    states = []
    for h in range(2):
        state = far_ref[h][:, 128:].astype(F32)
        state = follow(state, mid_ref[h])
        state = follow(state, near_ref[h])
        before = before_ref[h]
        states.append(state + dot3(before[:, :128], state) + before[:, 128:])
    for b in range(4):
        parts = []
        for h in range(2):
            cell = b * 2 + h
            out = dot2_right(r_ref[cell], states[h]) + o_ref[cell]
            mean = jnp.mean(out * out, axis=1, keepdims=True)
            parts.append((out * lax.rsqrt(mean + 1e-05)).astype(BF16))
        normed = jnp.concatenate(parts, 1)
        first, second = normed[:64], normed[64:]
        slot = pl.multiple_of(((4 - (y ^ b)) & 3) * 64, 64)
        keep_ref[pl.ds(slot, 64), :] = jnp.where(core == 0, first, second)
        send_ref[pl.ds(slot, 64), :] = jnp.where(core == 0, second, first)


HBM = pl.BlockSpec(memory_space=pltpu.HBM)
VMEM = pl.BlockSpec(memory_space=pltpu.VMEM)


def call(kernel, outs, arrays, flops, in_hbm=(), scratch=()):
    moved = sum(a.size * a.dtype.itemsize for a in (*in_hbm, *arrays, *outs))
    return pl.pallas_call(
        kernel,
        out_shape=[jax.ShapeDtypeStruct(a.shape, a.dtype) for a in outs],
        in_specs=[HBM] * len(in_hbm) + [VMEM] * len(arrays),
        out_specs=[VMEM] * len(outs),
        scratch_shapes=scratch,
        compiler_params=pltpu.CompilerParams(vmem_limit_bytes=VMEM_LIMIT),
        cost_estimate=pl.CostEstimate(flops=flops, bytes_accessed=moved, transcendentals=0),
        interpret=INTERPRET,
    )(*[pltpu.with_memory_space_constraint(a, pltpu.HBM) for a in in_hbm], *arrays)


def rows_product(own_rows, other_rows, own_w_ref, other_w_ref, first):
    columns = slice(first, first + CHUNK)
    out = dot(own_rows, own_w_ref[:, columns]) + dot(other_rows, other_w_ref[:, columns])
    return out.astype(BF16)


def send_kernel(part, keep_ref, joined_ref, own_w_ref, other_w_ref, near_ref, far_ref):
    weights = own_w_ref, other_w_ref, part * CHUNK
    near_ref[...] = rows_product(keep_ref[128:], joined_ref[128:], *weights)
    weights = own_w_ref, other_w_ref, 2048 + part * CHUNK
    far_ref[...] = rows_product(keep_ref[64:192], joined_ref[64:192], *weights)


def own_kernel(keep_ref, joined_ref, own_w_ref, other_w_ref, final_ref, passed_ref):
    for part in range(4):
        columns = slice(part * CHUNK, (part + 1) * CHUNK)
        weights = own_w_ref, other_w_ref, part * CHUNK
        if part < 2:
            out = rows_product(keep_ref[:128], joined_ref[:128], *weights)
        else:
            own_rows = jnp.concatenate([keep_ref[:64], keep_ref[192:]], 0)
            other_rows = jnp.concatenate([joined_ref[:64], joined_ref[192:]], 0)
            out = rows_product(own_rows, other_rows, *weights)
        final_ref[:, columns] = out[:64]
        passed_ref[:, columns] = out[64:]


def pair_kernel(part, passed_ref, sent_ref, out_ref):
    half = slice(0, 64) if part < 2 else slice(64, 128)
    own = passed_ref[:, part * CHUNK : (part + 1) * CHUNK].astype(F32)
    out_ref[...] = (own + sent_ref[half].astype(F32)).astype(BF16)


def sum_kernel(*refs):
    final_ref, out_ref = refs[0], refs[9]
    for part in range(4):
        columns = slice(part * CHUNK, (part + 1) * CHUNK)
        half = slice(64, 128) if part < 2 else slice(0, 64)
        total = final_ref[:, columns].astype(F32) + refs[1 + part][half].astype(F32)
        out_ref[:, columns] = (total + refs[5 + part][...].astype(F32)).astype(BF16)


def body(queries, keys, values, beta, reset_blocks, out_weight):
    k = keys.reshape(512, 256)
    v = values.reshape(512, 512)

    across = [(i, i ^ 1) for i in range(8)]
    other_weight = lax.ppermute(out_weight, "head", across)

    shaped = jax.ShapeDtypeStruct
    wu, prefix, scale, carry = call(
        terms_kernel,
        [
            shaped((8, 128, 384), F32),
            shaped((8, 128, 384), F32),
            shaped((8, 128), F32),
            shaped((2, 128, 384), BF16),
        ],
        [k, v],
        3_000_000_000,
        in_hbm=[reset_blocks, beta],
        scratch=[
            pltpu.SMEM((1, 2), jnp.int32),
            pltpu.VMEM((2, 512), F32),
            pltpu.SemaphoreType.DMA((2,)),
        ],
    )
    queries, carry = lax.optimization_barrier((queries, carry))
    response, own_out = call(
        response_kernel,
        [shaped((8, 128, 128), BF16), shaped((8, 128, 256), F32)],
        [queries.reshape(512, 256), k, scale, wu, prefix],
        2_000_000_000,
    )
    up = [(i, i - i % 8 + (i + 1) % 8) for i in range(32)]
    down = [(i, i - i % 8 + (i + 7) % 8) for i in range(32)]
    below, above = [carry], [carry]
    for step in range(3):
        below.append(lax.ppermute(below[-1], "seq", up))
        above.append(lax.ppermute(above[-1], "seq", down))
        if step == 0:
            below[1], above[1], response, own_out = lax.optimization_barrier(
                (below[1], above[1], response, own_out)
            )
    opposite = [
        lax.ppermute(below[3][0], "seq", up),
        lax.ppermute(above[3][1], "seq", down),
    ]
    before, total = call(
        group_kernel,
        [shaped((2, 128, 384), F32), shaped((2, 128, 384), BF16)],
        above + opposite + below[:0:-1],
        1_000_000_000,
    )
    received = [
        lax.ppermute(total, "seq", [(i, i + 8 * d) for i in range(32) if i + 8 * d < 32])
        for d in (3, 2, 1)
    ]
    keep, send = call(
        output_kernel,
        [shaped((256, 512), BF16), shaped((256, 512), BF16)],
        received + [before, response, own_out],
        500_000_000,
    )
    joined = lax.ppermute(send, "head", across)
    operands = [keep, joined, out_weight, other_weight]
    near = [(i, i ^ 2) for i in range(8)]
    far = [(i, i ^ 6) for i in range(8)]
    half = [shaped((128, CHUNK), BF16)] * 2
    routes = [near, near, far, far]
    sent = [None] * 4
    for part in range(2):
        to_near, to_far = call(
            functools.partial(send_kernel, part), half, operands, 500_000_000
        )
        operands[0], to_near, to_far = lax.optimization_barrier((operands[0], to_near, to_far))
        sent[part] = lax.ppermute(to_near, "head", near)
        sent[part + 2] = lax.ppermute(to_far, "head", far)
    final, passed = call(
        own_kernel, [shaped((64, 4096), BF16)] * 2, operands, 1_000_000_000
    )
    received = [None] * 4
    for part in (0, 2, 1, 3):
        (summed,) = call(
            functools.partial(pair_kernel, part),
            [shaped((64, CHUNK), BF16)],
            [passed, sent[part]],
            100_000,
        )
        received[part] = lax.ppermute(summed, "head", routes[3 - part])
    return call(sum_kernel, [shaped((64, 4096), BF16)], [final, *sent, *received], 1_000_000)[0]


def solution(mesh):
    return jax.shard_map(
        body,
        mesh=mesh,
        in_specs=(
            P("seq", "head", None),
            P("seq", "head", None),
            P("seq", "head", None),
            P("head", "seq"),
            P("seq", None),
            P("head", None),
        ),
        out_specs=P(("seq", "head"), None),
        check_vma=False,
    )
```

```python
import functools

import jax
import jax.numpy as jnp
from jax import lax
from jax.experimental import pallas as pl
from jax.experimental.pallas import tpu as pltpu
from jax.sharding import PartitionSpec as P

BLOCK = 128
INTERPRET = False
VMEM_LIMIT = 12 << 20
CHUNK = 1024
F32 = jnp.float32
BF16 = jnp.bfloat16


def split(x):
    high = x.astype(BF16)
    return high, (x - high.astype(F32)).astype(BF16)


def dot(a, b):
    return jnp.dot(a, b, preferred_element_type=F32)


def dot_t(a, b):
    return lax.dot_general(a, b, (((0,), (0,)), ((), ())), preferred_element_type=F32)


def dot_nt(a, b):
    return lax.dot_general(a, b, (((1,), (1,)), ((), ())), preferred_element_type=F32)


def dot3(a, b):
    a_high, a_low = split(a)
    b_high, b_low = split(b)
    left = jnp.concatenate([a_high, a_low], 1)
    right = jnp.concatenate([b_high, b_low], 1)
    both = dot(left, jnp.concatenate([right, right], 0))
    width = b.shape[1]
    return both[:, :width] + both[:, width:]


def dot2_right(a, b):
    b_high, b_low = split(b)
    return dot(jnp.concatenate([a, a], 1), jnp.concatenate([b_high, b_low], 0))


def dot2_left(a, b):
    a_high, a_low = split(a)
    return dot(jnp.concatenate([a_high, a_low], 1), jnp.concatenate([b, b], 0))


def square_ids(n):
    return lax.broadcasted_iota(jnp.int32, (n, n), 0), lax.broadcasted_iota(jnp.int32, (n, n), 1)


def head_rows(ref, b, head):
    row = lax.broadcasted_iota(jnp.int32, (BLOCK, 2 * BLOCK), 0)
    col = lax.broadcasted_iota(jnp.int32, (BLOCK, 2 * BLOCK), 1)
    chosen = jnp.where(col == 2 * row + head, 1.0, 0.0).astype(BF16)
    return dot(chosen, ref[b * 2 * BLOCK : (b + 1) * 2 * BLOCK]).astype(BF16)


def terms_kernel(head, resets_hbm, beta_hbm, k_ref, v_ref, *refs):
    wu_ref, prefix_ref, scale_ref, rows_ref, carry_ref, resets, beta_ref, sems = refs
    resets_copy = pltpu.make_async_copy(resets_hbm, resets, sems.at[0])
    beta_copy = pltpu.make_async_copy(beta_hbm, beta_ref, sems.at[1])
    beta_copy.start()
    resets_copy.start()
    row, col = square_ids(BLOCK)
    eye = row == col
    identity = jnp.where(eye, 1.0, 0.0).astype(F32)
    blocks = range(4)
    ks = [head_rows(k_ref, b, head) for b in blocks]
    vs = [head_rows(v_ref, b, head) for b in blocks]
    grams = [dot_nt(k, k) for k in ks]
    beta_copy.wait()
    lower, inv, r_cols, beta_rows, c_rows = [], [], [], [], []
    for b in blocks:
        gram = grams[b]
        diagonal = jnp.where(eye, gram, 0.0)
        r_col = lax.rsqrt(jnp.sum(diagonal, axis=1, keepdims=True) + 1e-06)
        r_row = lax.rsqrt(jnp.sum(diagonal, axis=0, keepdims=True) + 1e-06)
        beta_row = beta_ref[head : head + 1, b * BLOCK : (b + 1) * BLOCK]
        beta_col = jnp.sum(jnp.where(eye, beta_row, 0.0), axis=1, keepdims=True)
        low = jnp.where(row > col, (beta_col * r_col) * gram * r_row, 0.0)
        lower.append(low)
        inv.append(identity - jnp.where(row // 2 == col // 2, low, 0.0))
        r_cols.append(r_col)
        beta_rows.append(beta_row)
        c_rows.append(beta_row * r_row)
        scale_ref[b : b + 1, :] = r_row
        rows_ref[b] = ks[b]
    size = 2
    while size < BLOCK:
        joined = (row // (2 * size) == col // (2 * size)) & (row // size != col // size)
        half = [dot3(jnp.where(joined, lower[b], 0.0), inv[b]) for b in blocks]
        inv = [inv[b] - dot3(inv[b], half[b]) for b in blocks]
        size *= 2
    steps = []
    for b in blocks:
        decay = dot2_left(inv[b] * c_rows[b], ks[b])
        update = dot2_left(inv[b] * beta_rows[b], vs[b])
        wu = jnp.concatenate([decay, update], 1)
        wu_ref[b] = wu
        high, low = split(wu * r_cols[b])
        steps.append(
            dot_t(jnp.concatenate([ks[b], ks[b]], 0), jnp.concatenate([high, low], 0))
        )
    zeros = jnp.zeros((BLOCK, 256), F32)
    state = jnp.concatenate([identity, zeros], 1)
    resets_copy.wait()
    for b in blocks:
        starts = (resets[0, 0] == b) | (resets[0, 1] == b)
        kept = jnp.where(starts, 0.0, 1.0).astype(F32)
        before = state * kept
        prefix_ref[b] = before
        step = steps[b]
        added = jnp.concatenate([jnp.zeros((BLOCK, 128), F32), step[:, 128:]], 1)
        if b == 0:
            moved = jnp.concatenate([step[:, :128] * kept, zeros], 1)
        else:
            moved = dot3(step[:, :128], before)
        state = before - moved + added
    carry_ref[...] = jnp.concatenate([state[:, :128] - identity, state[:, 128:]], 1).astype(BF16)


def response_kernel(head, q_ref, k_ref, scale_ref, wu_ref, prefix_ref, r_ref, o_ref):
    row, col = square_ids(BLOCK)
    causal = row >= col
    for b in range(4):
        q = head_rows(q_ref, b, head)
        qf = q.astype(F32)
        rq = lax.rsqrt(jnp.sum(qf * qf, axis=1, keepdims=True) + 1e-06)
        scores = jnp.where(causal, rq * dot_nt(q, k_ref[b]) * scale_ref[b : b + 1, :], 0.0)
        local = dot3(scores, wu_ref[b])
        reach = qf * rq - local[:, :128]
        out = dot3(reach, prefix_ref[b])
        r_ref[b] = out[:, :128].astype(BF16)
        o_ref[b] = out[:, 128:] + local[:, 128:]


def follow(state, element):
    moved = dot2_right(element[:, :128], state)
    width = state.shape[1]
    added = element.astype(F32)
    if width == 256:
        added = added[:, 128:]
    else:
        added = jnp.concatenate([jnp.zeros((BLOCK, 128), F32), added[:, 128:]], 1)
    return state + moved + added


def group_kernel(*refs):
    elements, (before_ref, total_ref) = refs[:8], refs[8:]
    z = lax.axis_index("seq") % 8
    row, col = square_ids(BLOCK)
    identity = jnp.where(row == col, 1.0, 0.0).astype(F32)
    empty = jnp.concatenate([identity, jnp.zeros((BLOCK, 256), F32)], 1)
    state = after = empty
    for step in range(1, 8):
        wraps = z + step == 8
        if step > 1:
            after = jnp.where(wraps, state, after)
            state = jnp.where(wraps, empty, state)
        state = follow(state, elements[step][...])
    after = jnp.where(z == 0, state, after)
    state = jnp.where(z == 0, empty, state)
    before_ref[...] = jnp.concatenate([state[:, :128] - identity, state[:, 128:]], 1)
    through = follow(state, elements[0][...])
    total = dot3(after[:, :128], through)
    total_ref[...] = jnp.concatenate(
        [total[:, :128] - identity, total[:, 128:] + after[:, 128:]], 1
    ).astype(BF16)


def output_kernel(far_ref, mid_ref, near_ref, *refs):
    before_refs, r_refs, o_refs, (keep_ref, send_ref) = refs[:2], refs[2:4], refs[4:6], refs[6:]
    head = lax.axis_index("head")
    y, core = head // 2, head % 2
    states = []
    for h in range(2):
        state = far_ref[h][:, 128:].astype(F32)
        state = follow(state, mid_ref[h])
        state = follow(state, near_ref[h])
        before = before_refs[h][...]
        states.append(state + dot3(before[:, :128], state) + before[:, 128:])
    for b in range(4):
        parts = []
        for h in range(2):
            out = dot2_right(r_refs[h][b], states[h]) + o_refs[h][b]
            mean = jnp.mean(out * out, axis=1, keepdims=True)
            parts.append((out * lax.rsqrt(mean + 1e-05)).astype(BF16))
        normed = jnp.concatenate(parts, 1)
        first, second = normed[:64], normed[64:]
        slot = pl.multiple_of(((4 - (y ^ b)) & 3) * 64, 64)
        keep_ref[pl.ds(slot, 64), :] = jnp.where(core == 0, first, second)
        send_ref[pl.ds(slot, 64), :] = jnp.where(core == 0, second, first)


HBM = pl.BlockSpec(memory_space=pltpu.HBM)
VMEM = pl.BlockSpec(memory_space=pltpu.VMEM)


def call(kernel, outs, arrays, flops, in_hbm=(), scratch=()):
    moved = sum(a.size * a.dtype.itemsize for a in (*in_hbm, *arrays, *outs))
    return pl.pallas_call(
        kernel,
        out_shape=[jax.ShapeDtypeStruct(a.shape, a.dtype) for a in outs],
        in_specs=[HBM] * len(in_hbm) + [VMEM] * len(arrays),
        out_specs=[VMEM] * len(outs),
        scratch_shapes=scratch,
        compiler_params=pltpu.CompilerParams(vmem_limit_bytes=VMEM_LIMIT),
        cost_estimate=pl.CostEstimate(flops=flops, bytes_accessed=moved, transcendentals=0),
        interpret=INTERPRET,
    )(*[pltpu.with_memory_space_constraint(a, pltpu.HBM) for a in in_hbm], *arrays)


def rows_product(own_rows, other_rows, own_w_ref, other_w_ref, first):
    columns = slice(first, first + CHUNK)
    out = dot(own_rows, own_w_ref[:, columns]) + dot(other_rows, other_w_ref[:, columns])
    return out.astype(BF16)


def send_kernel(part, keep_ref, joined_ref, own_w_ref, other_w_ref, near_ref, far_ref):
    weights = own_w_ref, other_w_ref, part * CHUNK
    near_ref[...] = rows_product(keep_ref[128:], joined_ref[128:], *weights)
    weights = own_w_ref, other_w_ref, 2048 + part * CHUNK
    far_ref[...] = rows_product(keep_ref[64:192], joined_ref[64:192], *weights)


def own_kernel(keep_ref, joined_ref, own_w_ref, other_w_ref, final_ref, passed_ref):
    for part in range(4):
        columns = slice(part * CHUNK, (part + 1) * CHUNK)
        weights = own_w_ref, other_w_ref, part * CHUNK
        if part < 2:
            out = rows_product(keep_ref[:128], joined_ref[:128], *weights)
        else:
            own_rows = jnp.concatenate([keep_ref[:64], keep_ref[192:]], 0)
            other_rows = jnp.concatenate([joined_ref[:64], joined_ref[192:]], 0)
            out = rows_product(own_rows, other_rows, *weights)
        final_ref[:, columns] = out[:64]
        passed_ref[:, columns] = out[64:]


def pair_kernel(part, passed_ref, sent_ref, out_ref):
    half = slice(0, 64) if part < 2 else slice(64, 128)
    own = passed_ref[:, part * CHUNK : (part + 1) * CHUNK].astype(F32)
    out_ref[...] = (own + sent_ref[half].astype(F32)).astype(BF16)


def sum_kernel(*refs):
    final_ref, out_ref = refs[0], refs[9]
    for part in range(4):
        columns = slice(part * CHUNK, (part + 1) * CHUNK)
        half = slice(64, 128) if part < 2 else slice(0, 64)
        total = final_ref[:, columns].astype(F32) + refs[1 + part][half].astype(F32)
        out_ref[:, columns] = (total + refs[5 + part][...].astype(F32)).astype(BF16)


def body(queries, keys, values, beta, reset_blocks, out_weight):
    q = queries.reshape(1024, 128)
    k = keys.reshape(1024, 128)
    v = values.reshape(1024, 256)

    across = [(i, i ^ 1) for i in range(8)]
    shaped = jax.ShapeDtypeStruct
    terms = []
    for h in range(2):
        terms.append(
            list(call(
                functools.partial(terms_kernel, h),
                [
                    shaped((4, 128, 384), F32),
                    shaped((4, 128, 384), F32),
                    shaped((4, 128), F32),
                    shaped((4, 128, 128), BF16),
                    shaped((128, 384), BF16),
                ],
                [k, v],
                1_500_000_000,
                in_hbm=[reset_blocks, beta],
                scratch=[
                    pltpu.SMEM((1, 2), jnp.int32),
                    pltpu.VMEM((2, 512), F32),
                    pltpu.SemaphoreType.DMA((2,)),
                ],
            ))
        )
        if h == 0:
            k, swapped, terms[0][4] = lax.optimization_barrier((k, out_weight, terms[0][4]))
            other_weight = lax.ppermute(swapped, "head", across)
    up = [(i, i - i % 8 + (i + 1) % 8) for i in range(32)]
    down = [(i, i - i % 8 + (i + 7) % 8) for i in range(32)]
    below = [[terms[h][4]] for h in range(2)]
    above = [[terms[h][4]] for h in range(2)]
    for step in range(3):
        for h in range(2):
            below[h].append(lax.ppermute(below[h][-1], "seq", up))
            above[h].append(lax.ppermute(above[h][-1], "seq", down))
    opposite = [
        lax.ppermute(below[0][3], "seq", up),
        lax.ppermute(above[1][3], "seq", down),
    ]
    befores, totals = [], []
    for h in range(2):
        before, total = call(
            group_kernel,
            [shaped((128, 384), F32), shaped((128, 384), BF16)],
            above[h] + [opposite[h]] + below[h][:0:-1],
            500_000_000,
        )
        befores.append(before)
        totals.append(total)
    total = jnp.stack(totals)
    received = [
        lax.ppermute(total, "seq", [(i, i + 8 * d) for i in range(32) if i + 8 * d < 32])
        for d in (3, 2, 1)
    ]
    responses = []
    for h in range(2):
        wu, prefix, scale, rows, _ = terms[h]
        responses.append(
            call(
                functools.partial(response_kernel, h),
                [shaped((4, 128, 128), BF16), shaped((4, 128, 256), F32)],
                [q, rows, scale, wu, prefix],
                1_000_000_000,
            )
        )
    keep, send = call(
        output_kernel,
        [shaped((256, 512), BF16), shaped((256, 512), BF16)],
        received + befores + [r[0] for r in responses] + [r[1] for r in responses],
        500_000_000,
    )
    joined = lax.ppermute(send, "head", across)
    operands = [keep, joined, out_weight, other_weight]
    near = [(i, i ^ 2) for i in range(8)]
    far = [(i, i ^ 6) for i in range(8)]
    half = [shaped((128, CHUNK), BF16)] * 2
    routes = [near, near, far, far]
    sent = [None] * 4
    for part in range(2):
        to_near, to_far = call(
            functools.partial(send_kernel, part), half, operands, 500_000_000
        )
        operands[0], to_near, to_far = lax.optimization_barrier((operands[0], to_near, to_far))
        sent[part] = lax.ppermute(to_near, "head", near)
        sent[part + 2] = lax.ppermute(to_far, "head", far)
    final, passed = call(
        own_kernel, [shaped((64, 4096), BF16)] * 2, operands, 1_000_000_000
    )
    received = [None] * 4
    for part in (0, 2, 1, 3):
        (summed,) = call(
            functools.partial(pair_kernel, part),
            [shaped((64, CHUNK), BF16)],
            [passed, sent[part]],
            100_000,
        )
        received[part] = lax.ppermute(summed, "head", routes[3 - part])
    return call(sum_kernel, [shaped((64, 4096), BF16)], [final, *sent, *received], 1_000_000)[0]


def solution(mesh):
    return jax.shard_map(
        body,
        mesh=mesh,
        in_specs=(
            P("seq", "head", None),
            P("seq", "head", None),
            P("seq", "head", None),
            P("head", "seq"),
            P("seq", None),
            P("head", None),
        ),
        out_specs=P(("seq", "head"), None),
        check_vma=False,
    )
```

```python
import functools

import jax
import jax.numpy as jnp
from jax import lax
from jax.experimental import pallas as pl
from jax.experimental.pallas import tpu as pltpu
from jax.sharding import PartitionSpec as P

BLOCK = 128
INTERPRET = False
VMEM_LIMIT = 12 << 20
CHUNK = 1024
F32 = jnp.float32
BF16 = jnp.bfloat16


def split(x):
    high = x.astype(BF16)
    return high, (x - high.astype(F32)).astype(BF16)


def dot(a, b):
    return jnp.dot(a, b, preferred_element_type=F32)


def dot_t(a, b):
    return lax.dot_general(a, b, (((0,), (0,)), ((), ())), preferred_element_type=F32)


def dot_nt(a, b):
    return lax.dot_general(a, b, (((1,), (1,)), ((), ())), preferred_element_type=F32)


def dot3(a, b):
    a_high, a_low = split(a)
    b_high, b_low = split(b)
    left = jnp.concatenate([a_high, a_low], 1)
    right = jnp.concatenate([b_high, b_low], 1)
    both = dot(left, jnp.concatenate([right, right], 0))
    width = b.shape[1]
    return both[:, :width] + both[:, width:]


def dot2_right(a, b):
    b_high, b_low = split(b)
    return dot(jnp.concatenate([a, a], 1), jnp.concatenate([b_high, b_low], 0))


def dot2_left(a, b):
    a_high, a_low = split(a)
    return dot(jnp.concatenate([a_high, a_low], 1), jnp.concatenate([b, b], 0))


def square_ids(n):
    return lax.broadcasted_iota(jnp.int32, (n, n), 0), lax.broadcasted_iota(jnp.int32, (n, n), 1)


def head_rows(rows, width, place):
    row = lax.broadcasted_iota(jnp.int32, (BLOCK, width * BLOCK), 0)
    col = lax.broadcasted_iota(jnp.int32, (BLOCK, width * BLOCK), 1)
    chosen = jnp.where(col == width * row + place, 1.0, 0.0).astype(BF16)
    return dot(chosen, rows).astype(BF16)


CELLS = [(b, h) for b in range(4) for h in range(2)]


def after_map(first, second):
    added = jnp.concatenate([jnp.zeros((BLOCK, 128), F32), second[:, 128:]], 1)
    return dot3(second[:, :128], first) + added


def terms_kernel(resets_hbm, beta_hbm, k_hbm, v_ref, *refs):
    wu_ref, prefix_ref, scale_ref, rows_ref, carry_ref = refs[:5]
    resets, beta_ref, k_ref, sems = refs[5:]
    k_copy = pltpu.make_async_copy(k_hbm, k_ref, sems.at[2])
    resets_copy = pltpu.make_async_copy(resets_hbm, resets, sems.at[0])
    beta_copy = pltpu.make_async_copy(beta_hbm, beta_ref, sems.at[1])
    k_copy.start()
    beta_copy.start()
    resets_copy.start()
    row, col = square_ids(BLOCK)
    eye = row == col
    identity = jnp.where(eye, 1.0, 0.0).astype(F32)
    ks, vs, grams = {}, {}, {}
    k_copy.wait()
    for b, h in CELLS:
        ks[b, h] = head_rows(k_ref[b * 2 * BLOCK : (b + 1) * 2 * BLOCK], 2, h)
        vs[b, h] = v_ref[b * BLOCK : (b + 1) * BLOCK, h * 256 : (h + 1) * 256]
        rows_ref[b * 2 + h] = ks[b, h]
    for cell in CELLS:
        grams[cell] = dot_nt(ks[cell], ks[cell])
    beta_copy.wait()
    lower, inv, r_cols, beta_rows, c_rows = {}, {}, {}, {}, {}
    for b, h in CELLS:
        gram = grams[b, h]
        diagonal = jnp.where(eye, gram, 0.0)
        r_col = lax.rsqrt(jnp.sum(diagonal, axis=1, keepdims=True) + 1e-06)
        r_row = lax.rsqrt(jnp.sum(diagonal, axis=0, keepdims=True) + 1e-06)
        beta_row = beta_ref[h : h + 1, b * BLOCK : (b + 1) * BLOCK]
        beta_col = jnp.sum(jnp.where(eye, beta_row, 0.0), axis=1, keepdims=True)
        low = jnp.where(row > col, (beta_col * r_col) * gram * r_row, 0.0)
        lower[b, h] = low
        inv[b, h] = identity - jnp.where(row // 2 == col // 2, low, 0.0)
        r_cols[b, h] = r_col
        beta_rows[b, h] = beta_row
        c_rows[b, h] = beta_row * r_row
        scale_ref[b * 2 + h : b * 2 + h + 1, :] = r_row
    size = 2
    while size < BLOCK:
        joined = (row // (4 * size) == col // (4 * size)) & (row // size != col // size)
        links, squares, odds = {}, {}, {}
        for cell in CELLS:
            links[cell] = dot3(inv[cell], jnp.where(joined, lower[cell], 0.0))
        for cell in CELLS:
            squares[cell] = dot3(links[cell], links[cell])
            odds[cell] = inv[cell] - dot3(links[cell], inv[cell])
        for cell in CELLS:
            inv[cell] = odds[cell] + dot3(squares[cell], odds[cell])
        size *= 4
    resets_copy.wait()
    maps = {}
    kept = []
    for b in range(4):
        starts = (resets[0, 0] == b) | (resets[0, 1] == b)
        kept.append(jnp.where(starts, 0.0, 1.0).astype(F32))
    for b, h in CELLS:
        cell = (b, h)
        decay = dot2_left(inv[cell] * c_rows[cell], ks[cell])
        update = dot2_left(inv[cell] * beta_rows[cell], vs[cell])
        wu = jnp.concatenate([decay, update], 1)
        wu_ref[b * 2 + h] = wu
        high, low = split(wu * r_cols[cell])
        step = dot_t(jnp.concatenate([ks[cell], ks[cell]], 0), jnp.concatenate([high, low], 0))
        maps[cell] = jnp.concatenate([(identity - step[:, :128]) * kept[b], step[:, 128:]], 1)
    zeros = jnp.zeros((BLOCK, 256), F32)
    for h in range(2):
        first = after_map(maps[0, h], maps[1, h])
        last = after_map(maps[2, h], maps[3, h])
        whole = after_map(first, last)
        carry_ref[h] = jnp.concatenate(
            [whole[:, :128] - identity, whole[:, 128:]], 1
        ).astype(BF16)
        prefix_ref[h] = jnp.concatenate([identity, zeros], 1) * kept[0]
        prefix_ref[2 + h] = maps[0, h] * kept[1]
        prefix_ref[4 + h] = first * kept[2]
        prefix_ref[6 + h] = after_map(first, maps[2, h]) * kept[3]


def response_kernel(q_ref, k_ref, scale_ref, wu_ref, prefix_ref, r_ref, o_ref):
    row, col = square_ids(BLOCK)
    causal = row >= col
    for b, h in CELLS:
        cell = b * 2 + h
        q = head_rows(q_ref[b * 2 * BLOCK : (b + 1) * 2 * BLOCK], 2, h)
        qf = q.astype(F32)
        rq = lax.rsqrt(jnp.sum(qf * qf, axis=1, keepdims=True) + 1e-06)
        scores = rq * dot_nt(q, k_ref[cell]) * scale_ref[cell : cell + 1, :]
        local = dot3(jnp.where(causal, scores, 0.0), wu_ref[cell])
        reach = qf * rq - local[:, :128]
        out = dot3(reach, prefix_ref[cell])
        r_ref[cell] = out[:, :128].astype(BF16)
        o_ref[cell] = out[:, 128:] + local[:, 128:]


def follow(state, element):
    moved = dot2_right(element[:, :128], state)
    width = state.shape[1]
    added = element.astype(F32)
    if width == 256:
        added = added[:, 128:]
    else:
        added = jnp.concatenate([jnp.zeros((BLOCK, 128), F32), added[:, 128:]], 1)
    return state + moved + added


def group_kernel(*refs):
    refs, (before_ref, total_ref) = refs[:9], refs[9:]
    elements = [(ref.at[0], ref.at[1]) for ref in refs[:4] + refs[6:]]
    elements.insert(4, refs[4:6])
    row, col = square_ids(BLOCK)
    identity = jnp.where(row == col, 1.0, 0.0).astype(F32)
    empty = jnp.concatenate([identity, jnp.zeros((BLOCK, 256), F32)], 1)
    z = lax.axis_index("seq") % 8
    state = {h: empty for h in range(2)}
    after = {h: empty for h in range(2)}
    for step in range(1, 8):
        wraps = z + step == 8
        for h in range(2):
            if step > 1:
                after[h] = jnp.where(wraps, state[h], after[h])
                state[h] = jnp.where(wraps, empty, state[h])
            state[h] = follow(state[h], elements[step][h][...])
    for h in range(2):
        after[h] = jnp.where(z == 0, state[h], after[h])
        state[h] = jnp.where(z == 0, empty, state[h])
        before_ref[h] = jnp.concatenate([state[h][:, :128] - identity, state[h][:, 128:]], 1)
        through = follow(state[h], elements[0][h][...])
        total = dot3(after[h][:, :128], through)
        total_ref[h] = jnp.concatenate(
            [total[:, :128] - identity, total[:, 128:] + after[h][:, 128:]], 1
        ).astype(BF16)


def pass_kernel(own_ref, peer_ref, out_ref):
    odd = (lax.axis_index("seq") // 8) % 2 == 1
    for h in range(2):
        early = jnp.where(odd, peer_ref[h], own_ref[h])
        late = jnp.where(odd, own_ref[h], peer_ref[h])
        out_ref[h] = follow(early[:, 128:].astype(F32), late).astype(BF16)


def output_kernel(peer_ref, passed_ref, before_ref, r_ref, o_ref, keep_ref, send_ref):
    head = lax.axis_index("head")
    y, core = head // 2, head % 2
    odd = (lax.axis_index("seq") // 8) % 2 == 1
    states = []
    for h in range(2):
        state = passed_ref[h].astype(F32)
        state = jnp.where(odd, follow(state, peer_ref[h]), state)
        before = before_ref[h]
        states.append(state + dot3(before[:, :128], state) + before[:, 128:])
    for b in range(4):
        parts = []
        for h in range(2):
            cell = b * 2 + h
            out = dot2_right(r_ref[cell], states[h]) + o_ref[cell]
            mean = jnp.mean(out * out, axis=1, keepdims=True)
            parts.append((out * lax.rsqrt(mean + 1e-05)).astype(BF16))
        normed = jnp.concatenate(parts, 1)
        first, second = normed[:64], normed[64:]
        slot = pl.multiple_of(((4 - (y ^ b)) & 3) * 64, 64)
        keep_ref[pl.ds(slot, 64), :] = jnp.where(core == 0, first, second)
        send_ref[pl.ds(slot, 64), :] = jnp.where(core == 0, second, first)


HBM = pl.BlockSpec(memory_space=pltpu.HBM)
VMEM = pl.BlockSpec(memory_space=pltpu.VMEM)


def call(kernel, outs, arrays, flops, in_hbm=(), scratch=()):
    moved = sum(a.size * a.dtype.itemsize for a in (*in_hbm, *arrays, *outs))
    return pl.pallas_call(
        kernel,
        out_shape=[jax.ShapeDtypeStruct(a.shape, a.dtype) for a in outs],
        in_specs=[HBM] * len(in_hbm) + [VMEM] * len(arrays),
        out_specs=[VMEM] * len(outs),
        scratch_shapes=scratch,
        compiler_params=pltpu.CompilerParams(vmem_limit_bytes=VMEM_LIMIT),
        cost_estimate=pl.CostEstimate(flops=flops, bytes_accessed=moved, transcendentals=0),
        interpret=INTERPRET,
    )(*[pltpu.with_memory_space_constraint(a, pltpu.HBM) for a in in_hbm], *arrays)


def rows_product(own_rows, other_rows, own_w_ref, other_w_ref, first):
    columns = slice(first, first + CHUNK)
    out = dot(own_rows, own_w_ref[:, columns]) + dot(other_rows, other_w_ref[:, columns])
    return out.astype(BF16)


def send_kernel(part, keep_ref, joined_ref, own_w_ref, other_w_ref, near_ref, far_ref):
    weights = own_w_ref, other_w_ref, part * CHUNK
    near_ref[...] = rows_product(keep_ref[128:], joined_ref[128:], *weights)
    weights = own_w_ref, other_w_ref, 2048 + part * CHUNK
    far_ref[...] = rows_product(keep_ref[64:192], joined_ref[64:192], *weights)


def own_kernel(keep_ref, joined_ref, own_w_ref, other_w_ref, final_ref, passed_ref):
    for part in range(4):
        columns = slice(part * CHUNK, (part + 1) * CHUNK)
        weights = own_w_ref, other_w_ref, part * CHUNK
        if part < 2:
            out = rows_product(keep_ref[:128], joined_ref[:128], *weights)
        else:
            own_rows = jnp.concatenate([keep_ref[:64], keep_ref[192:]], 0)
            other_rows = jnp.concatenate([joined_ref[:64], joined_ref[192:]], 0)
            out = rows_product(own_rows, other_rows, *weights)
        final_ref[:, columns] = out[:64]
        passed_ref[:, columns] = out[64:]


def pair_kernel(part, passed_ref, sent_ref, out_ref):
    half = slice(0, 64) if part < 2 else slice(64, 128)
    own = passed_ref[:, part * CHUNK : (part + 1) * CHUNK].astype(F32)
    out_ref[...] = (own + sent_ref[half].astype(F32)).astype(BF16)


def sum_kernel(*refs):
    final_ref, out_ref = refs[0], refs[9]
    for part in range(4):
        columns = slice(part * CHUNK, (part + 1) * CHUNK)
        half = slice(64, 128) if part < 2 else slice(0, 64)
        total = final_ref[:, columns].astype(F32) + refs[1 + part][half].astype(F32)
        out_ref[:, columns] = (total + refs[5 + part][...].astype(F32)).astype(BF16)


def body(queries, keys, values, beta, reset_blocks, out_weight):
    q = queries.reshape(1024, 128)
    k = keys.reshape(1024, 128)
    v = values.reshape(512, 512)

    across = [(i, i ^ 1) for i in range(8)]
    other_weight = lax.ppermute(out_weight, "head", across)

    shaped = jax.ShapeDtypeStruct
    wu, prefix, scale, rows, carry = call(
        terms_kernel,
        [
            shaped((8, 128, 384), F32),
            shaped((8, 128, 384), F32),
            shaped((8, 128), F32),
            shaped((8, 128, 128), BF16),
            shaped((2, 128, 384), BF16),
        ],
        [v],
        3_000_000_000,
        in_hbm=[reset_blocks, beta, k],
        scratch=[
            pltpu.SMEM((1, 2), jnp.int32),
            pltpu.VMEM((2, 512), F32),
            pltpu.VMEM((1024, 128), BF16),
            pltpu.SemaphoreType.DMA((3,)),
        ],
    )
    up = [(i, i - i % 8 + (i + 1) % 8) for i in range(32)]
    down = [(i, i - i % 8 + (i + 7) % 8) for i in range(32)]
    below, above = [carry], [carry]
    for step in range(3):
        below.append(lax.ppermute(below[-1], "seq", up))
        above.append(lax.ppermute(above[-1], "seq", down))
    opposite = [
        lax.ppermute(below[3][0], "seq", up),
        lax.ppermute(above[3][1], "seq", down),
    ]
    before, total = call(
        group_kernel,
        [shaped((2, 128, 384), F32), shaped((2, 128, 384), BF16)],
        above + opposite + below[:0:-1],
        1_000_000_000,
    )
    peer = lax.ppermute(total, "seq", [(i, i ^ 8) for i in range(32)])
    response, own_out = call(
        response_kernel,
        [shaped((8, 128, 128), BF16), shaped((8, 128, 256), F32)],
        [q, rows, scale, wu, prefix],
        2_000_000_000,
    )
    peer, response, own_out = lax.optimization_barrier((peer, response, own_out))
    (joint,) = call(pass_kernel, [shaped((2, 128, 256), BF16)], [total, peer], 100_000_000)
    passed = lax.ppermute(
        joint, "seq", [(z + 8 * x, z + 8 * (3 - x)) for x in (0, 1) for z in range(8)]
    )
    keep, send = call(
        output_kernel,
        [shaped((256, 512), BF16), shaped((256, 512), BF16)],
        [peer, passed, before, response, own_out],
        500_000_000,
    )
    joined = lax.ppermute(send, "head", across)
    operands = [keep, joined, out_weight, other_weight]
    near = [(i, i ^ 2) for i in range(8)]
    far = [(i, i ^ 6) for i in range(8)]
    half = [shaped((128, CHUNK), BF16)] * 2
    routes = [near, near, far, far]
    sent = [None] * 4
    for part in range(2):
        to_near, to_far = call(
            functools.partial(send_kernel, part), half, operands, 500_000_000
        )
        operands[0], to_near, to_far = lax.optimization_barrier((operands[0], to_near, to_far))
        sent[part] = lax.ppermute(to_near, "head", near)
        sent[part + 2] = lax.ppermute(to_far, "head", far)
    final, passed = call(
        own_kernel, [shaped((64, 4096), BF16)] * 2, operands, 1_000_000_000
    )
    received = [None] * 4
    for part in (0, 2, 1, 3):
        (summed,) = call(
            functools.partial(pair_kernel, part),
            [shaped((64, CHUNK), BF16)],
            [passed, sent[part]],
            100_000,
        )
        received[part] = lax.ppermute(summed, "head", routes[3 - part])
    return call(sum_kernel, [shaped((64, 4096), BF16)], [final, *sent, *received], 1_000_000)[0]


def solution(mesh):
    return jax.shard_map(
        body,
        mesh=mesh,
        in_specs=(
            P("seq", "head", None),
            P("seq", "head", None),
            P("seq", "head", None),
            P("head", "seq"),
            P("seq", None),
            P("head", None),
        ),
        out_specs=P(("seq", "head"), None),
        check_vma=False,
    )
```

```python
import functools

import jax
import jax.numpy as jnp
from jax import lax
from jax.experimental import pallas as pl
from jax.experimental.pallas import tpu as pltpu
from jax.sharding import PartitionSpec as P

BLOCK = 128
INTERPRET = False
VMEM_LIMIT = 12 << 20
CHUNK = 1024
F32 = jnp.float32
BF16 = jnp.bfloat16


def split(x):
    high = x.astype(BF16)
    return high, (x - high.astype(F32)).astype(BF16)


def dot(a, b):
    return jnp.dot(a, b, preferred_element_type=F32)


def dot_t(a, b):
    return lax.dot_general(a, b, (((0,), (0,)), ((), ())), preferred_element_type=F32)


def dot_nt(a, b):
    return lax.dot_general(a, b, (((1,), (1,)), ((), ())), preferred_element_type=F32)


def dot3(a, b):
    a_high, a_low = split(a)
    b_high, b_low = split(b)
    left = jnp.concatenate([a_high, a_low], 1)
    right = jnp.concatenate([b_high, b_low], 1)
    both = dot(left, jnp.concatenate([right, right], 0))
    width = b.shape[1]
    return both[:, :width] + both[:, width:]


def dot2_right(a, b):
    b_high, b_low = split(b)
    return dot(jnp.concatenate([a, a], 1), jnp.concatenate([b_high, b_low], 0))


def dot2_left(a, b):
    a_high, a_low = split(a)
    return dot(jnp.concatenate([a_high, a_low], 1), jnp.concatenate([b, b], 0))


def square_ids(n):
    return lax.broadcasted_iota(jnp.int32, (n, n), 0), lax.broadcasted_iota(jnp.int32, (n, n), 1)


def head_rows(rows, width, place):
    row = lax.broadcasted_iota(jnp.int32, (BLOCK, width * BLOCK), 0)
    col = lax.broadcasted_iota(jnp.int32, (BLOCK, width * BLOCK), 1)
    chosen = jnp.where(col == width * row + place, 1.0, 0.0).astype(BF16)
    return dot(chosen, rows).astype(BF16)


CELLS = [(b, h) for b in range(4) for h in range(2)]


def after_map(first, second):
    added = jnp.concatenate([jnp.zeros((BLOCK, 128), F32), second[:, 128:]], 1)
    return dot3(second[:, :128], first) + added


def terms_kernel(resets_hbm, beta_hbm, k_hbm, v_ref, *refs):
    wu_ref, prefix_ref, scale_ref, rows_ref, carry_ref = refs[:5]
    resets, beta_ref, k_ref, sems = refs[5:]
    k_copy = pltpu.make_async_copy(k_hbm, k_ref, sems.at[2])
    resets_copy = pltpu.make_async_copy(resets_hbm, resets, sems.at[0])
    beta_copy = pltpu.make_async_copy(beta_hbm, beta_ref, sems.at[1])
    k_copy.start()
    beta_copy.start()
    resets_copy.start()
    row, col = square_ids(BLOCK)
    eye = row == col
    identity = jnp.where(eye, 1.0, 0.0).astype(F32)
    ks, vs, grams = {}, {}, {}
    k_copy.wait()
    for b, h in CELLS:
        ks[b, h] = head_rows(k_ref[b * 2 * BLOCK : (b + 1) * 2 * BLOCK], 2, h)
        vs[b, h] = v_ref[b * BLOCK : (b + 1) * BLOCK, h * 256 : (h + 1) * 256]
        rows_ref[b * 2 + h] = ks[b, h]
    for cell in CELLS:
        grams[cell] = dot_nt(ks[cell], ks[cell])
    beta_copy.wait()
    lower, inv, r_cols, beta_rows, c_rows = {}, {}, {}, {}, {}
    for b, h in CELLS:
        gram = grams[b, h]
        diagonal = jnp.where(eye, gram, 0.0)
        r_col = lax.rsqrt(jnp.sum(diagonal, axis=1, keepdims=True) + 1e-06)
        r_row = lax.rsqrt(jnp.sum(diagonal, axis=0, keepdims=True) + 1e-06)
        beta_row = beta_ref[h : h + 1, b * BLOCK : (b + 1) * BLOCK]
        beta_col = jnp.sum(jnp.where(eye, beta_row, 0.0), axis=1, keepdims=True)
        low = jnp.where(row > col, (beta_col * r_col) * gram * r_row, 0.0)
        lower[b, h] = low
        inv[b, h] = identity - jnp.where(row // 2 == col // 2, low, 0.0)
        r_cols[b, h] = r_col
        beta_rows[b, h] = beta_row
        c_rows[b, h] = beta_row * r_row
        scale_ref[b * 2 + h : b * 2 + h + 1, :] = r_row
    size = 2
    while size < BLOCK:
        joined = (row // (4 * size) == col // (4 * size)) & (row // size != col // size)
        links, squares, odds = {}, {}, {}
        for cell in CELLS:
            links[cell] = dot3(inv[cell], jnp.where(joined, lower[cell], 0.0))
        for cell in CELLS:
            squares[cell] = dot3(links[cell], links[cell])
            odds[cell] = inv[cell] - dot3(links[cell], inv[cell])
        for cell in CELLS:
            inv[cell] = odds[cell] + dot3(squares[cell], odds[cell])
        size *= 4
    resets_copy.wait()
    maps = {}
    kept = []
    for b in range(4):
        starts = (resets[0, 0] == b) | (resets[0, 1] == b)
        kept.append(jnp.where(starts, 0.0, 1.0).astype(F32))
    for b, h in CELLS:
        cell = (b, h)
        decay = dot2_left(inv[cell] * c_rows[cell], ks[cell])
        update = dot2_left(inv[cell] * beta_rows[cell], vs[cell])
        wu = jnp.concatenate([decay, update], 1)
        wu_ref[b * 2 + h] = wu
        high, low = split(wu * r_cols[cell])
        step = dot_t(jnp.concatenate([ks[cell], ks[cell]], 0), jnp.concatenate([high, low], 0))
        maps[cell] = jnp.concatenate([(identity - step[:, :128]) * kept[b], step[:, 128:]], 1)
    zeros = jnp.zeros((BLOCK, 256), F32)
    for h in range(2):
        first = after_map(maps[0, h], maps[1, h])
        last = after_map(maps[2, h], maps[3, h])
        whole = after_map(first, last)
        carry_ref[h] = jnp.concatenate(
            [whole[:, :128] - identity, whole[:, 128:]], 1
        ).astype(BF16)
        prefix_ref[h] = jnp.concatenate([identity, zeros], 1) * kept[0]
        prefix_ref[2 + h] = maps[0, h] * kept[1]
        prefix_ref[4 + h] = first * kept[2]
        prefix_ref[6 + h] = after_map(first, maps[2, h]) * kept[3]


def response_kernel(q_ref, k_ref, scale_ref, wu_ref, prefix_ref, keep_ref, send_ref):
    row, col = square_ids(BLOCK)
    causal = row >= col
    core = lax.axis_index("head") % 2
    for b, h in CELLS:
        cell = b * 2 + h
        q = head_rows(q_ref[b * 2 * BLOCK : (b + 1) * 2 * BLOCK], 2, h)
        qf = q.astype(F32)
        rq = lax.rsqrt(jnp.sum(qf * qf, axis=1, keepdims=True) + 1e-06)
        scores = rq * dot_nt(q, k_ref[cell]) * scale_ref[cell : cell + 1, :]
        local = dot3(jnp.where(causal, scores, 0.0), wu_ref[cell])
        reach = qf * rq - local[:, :128]
        out = dot3(reach, prefix_ref[cell])
        out = jnp.concatenate([out[:, :128], out[:, 128:] + local[:, 128:]], 1)
        keep_ref[cell] = jnp.where(core == 0, out[:64], out[64:])
        send_ref[cell] = jnp.where(core == 0, out[64:], out[:64])


def follow(state, element):
    moved = dot2_right(element[:, :128], state)
    width = state.shape[1]
    added = element.astype(F32)
    if width == 256:
        added = added[:, 128:]
    else:
        added = jnp.concatenate([jnp.zeros((BLOCK, 128), F32), added[:, 128:]], 1)
    return state + moved + added


def group_kernel(*refs):
    refs, (before_ref, total_ref) = refs[:9], refs[9:]
    elements = [[ref.at[h] for h in range(4)] for ref in refs[:4] + refs[6:]]
    elements.insert(4, [refs[4].at[0], refs[4].at[1], refs[5].at[0], refs[5].at[1]])
    row, col = square_ids(BLOCK)
    identity = jnp.where(row == col, 1.0, 0.0).astype(F32)
    empty = jnp.concatenate([identity, jnp.zeros((BLOCK, 256), F32)], 1)
    z = lax.axis_index("seq") % 8
    state = {h: empty for h in range(4)}
    after = {h: empty for h in range(4)}
    for step in range(1, 8):
        wraps = z + step == 8
        for h in range(4):
            if step > 1:
                after[h] = jnp.where(wraps, state[h], after[h])
                state[h] = jnp.where(wraps, empty, state[h])
            state[h] = follow(state[h], elements[step][h][...])
    for h in range(4):
        after[h] = jnp.where(z == 0, state[h], after[h])
        state[h] = jnp.where(z == 0, empty, state[h])
        before_ref[h] = jnp.concatenate([state[h][:, :128] - identity, state[h][:, 128:]], 1)
        through = follow(state[h], elements[0][h][...])
        total = dot3(after[h][:, :128], through)
        total_ref[h] = jnp.concatenate(
            [total[:, :128] - identity, total[:, 128:] + after[h][:, 128:]], 1
        ).astype(BF16)


def pass_kernel(own_ref, peer_ref, out_ref):
    odd = (lax.axis_index("seq") // 8) % 2 == 1
    for h in range(4):
        early = jnp.where(odd, peer_ref[h], own_ref[h])
        late = jnp.where(odd, own_ref[h], peer_ref[h])
        out_ref[h] = follow(early[:, 128:].astype(F32), late).astype(BF16)


def state_kernel(peer_ref, passed_ref, before_ref, out_ref):
    odd = (lax.axis_index("seq") // 8) % 2 == 1
    for h in range(4):
        state = passed_ref[h].astype(F32)
        state = jnp.where(odd, follow(state, peer_ref[h]), state)
        before = before_ref[h]
        state = state + dot3(before[:, :128], state) + before[:, 128:]
        out_ref[h] = state.astype(BF16)


def output_kernel(state_ref, received_ref, own_ref, other_ref, keep_ref, joined_ref):
    head = lax.axis_index("head")
    y, core = head // 2, head % 2
    for source_ref, out_ref, at in ((own_ref, keep_ref, 0), (other_ref, joined_ref, 2)):
        states = [
            jnp.where(core == 1, state_ref[at + h], received_ref[2 - at + h]) for h in range(2)
        ]
        for b in range(4):
            parts = []
            for h in range(2):
                source = source_ref[b * 2 + h]
                out = dot2_left(source[:, :128], states[h]) + source[:, 128:]
                mean = jnp.mean(out * out, axis=1, keepdims=True)
                parts.append((out * lax.rsqrt(mean + 1e-05)).astype(BF16))
            slot = pl.multiple_of(((4 - (y ^ b)) & 3) * 64, 64)
            out_ref[pl.ds(slot, 64), :] = jnp.concatenate(parts, 1)


HBM = pl.BlockSpec(memory_space=pltpu.HBM)
VMEM = pl.BlockSpec(memory_space=pltpu.VMEM)


def call(kernel, outs, arrays, flops, in_hbm=(), scratch=()):
    moved = sum(a.size * a.dtype.itemsize for a in (*in_hbm, *arrays, *outs))
    return pl.pallas_call(
        kernel,
        out_shape=[jax.ShapeDtypeStruct(a.shape, a.dtype) for a in outs],
        in_specs=[HBM] * len(in_hbm) + [VMEM] * len(arrays),
        out_specs=[VMEM] * len(outs),
        scratch_shapes=scratch,
        compiler_params=pltpu.CompilerParams(vmem_limit_bytes=VMEM_LIMIT),
        cost_estimate=pl.CostEstimate(flops=flops, bytes_accessed=moved, transcendentals=0),
        interpret=INTERPRET,
    )(*[pltpu.with_memory_space_constraint(a, pltpu.HBM) for a in in_hbm], *arrays)


def rows_product(own_rows, other_rows, own_w_ref, other_w_ref, first):
    columns = slice(first, first + CHUNK)
    out = dot(own_rows, own_w_ref[:, columns]) + dot(other_rows, other_w_ref[:, columns])
    return out.astype(BF16)


def send_kernel(part, keep_ref, joined_ref, own_w_ref, other_w_ref, near_ref, far_ref):
    weights = own_w_ref, other_w_ref, part * CHUNK
    near_ref[...] = rows_product(keep_ref[128:], joined_ref[128:], *weights)
    weights = own_w_ref, other_w_ref, 2048 + part * CHUNK
    far_ref[...] = rows_product(keep_ref[64:192], joined_ref[64:192], *weights)


def own_kernel(keep_ref, joined_ref, own_w_ref, other_w_ref, final_ref, passed_ref):
    for part in range(4):
        columns = slice(part * CHUNK, (part + 1) * CHUNK)
        weights = own_w_ref, other_w_ref, part * CHUNK
        if part < 2:
            out = rows_product(keep_ref[:128], joined_ref[:128], *weights)
        else:
            own_rows = jnp.concatenate([keep_ref[:64], keep_ref[192:]], 0)
            other_rows = jnp.concatenate([joined_ref[:64], joined_ref[192:]], 0)
            out = rows_product(own_rows, other_rows, *weights)
        final_ref[:, columns] = out[:64]
        passed_ref[:, columns] = out[64:]


def pair_kernel(part, passed_ref, sent_ref, out_ref):
    half = slice(0, 64) if part < 2 else slice(64, 128)
    own = passed_ref[:, part * CHUNK : (part + 1) * CHUNK].astype(F32)
    out_ref[...] = (own + sent_ref[half].astype(F32)).astype(BF16)


def sum_kernel(*refs):
    final_ref, out_ref = refs[0], refs[9]
    for part in range(4):
        columns = slice(part * CHUNK, (part + 1) * CHUNK)
        half = slice(64, 128) if part < 2 else slice(0, 64)
        total = final_ref[:, columns].astype(F32) + refs[1 + part][half].astype(F32)
        out_ref[:, columns] = (total + refs[5 + part][...].astype(F32)).astype(BF16)


def body(queries, keys, values, beta, reset_blocks, out_weight):
    q = queries.reshape(1024, 128)
    k = keys.reshape(1024, 128)
    v = values.reshape(512, 512)

    across = [(i, i ^ 1) for i in range(8)]
    other_weight = lax.ppermute(out_weight, "head", across)

    shaped = jax.ShapeDtypeStruct
    wu, prefix, scale, rows, carry = call(
        terms_kernel,
        [
            shaped((8, 128, 384), F32),
            shaped((8, 128, 384), F32),
            shaped((8, 128), F32),
            shaped((8, 128, 128), BF16),
            shaped((2, 128, 384), BF16),
        ],
        [v],
        3_000_000_000,
        in_hbm=[reset_blocks, beta, k],
        scratch=[
            pltpu.SMEM((1, 2), jnp.int32),
            pltpu.VMEM((2, 512), F32),
            pltpu.VMEM((1024, 128), BF16),
            pltpu.SemaphoreType.DMA((3,)),
        ],
    )
    to_core_one = lax.ppermute(carry, "head", [(i, i + 1) for i in range(0, 8, 2)])
    carry = jnp.concatenate([carry, to_core_one], 0)

    def moved(x, route):
        pairs = [(s * 8 + h, d * 8 + h) for s, d in route for h in range(1, 8, 2)]
        return lax.ppermute(x, ("seq", "head"), pairs)

    up = [(i, i - i % 8 + (i + 1) % 8) for i in range(32)]
    down = [(i, i - i % 8 + (i + 7) % 8) for i in range(32)]
    below, above = [carry], [carry]
    for step in range(3):
        below.append(moved(below[-1], up))
        above.append(moved(above[-1], down))
    opposite = [moved(below[3][:2], up), moved(above[3][2:], down)]
    before, total = call(
        group_kernel,
        [shaped((4, 128, 384), F32), shaped((4, 128, 384), BF16)],
        above + opposite + below[:0:-1],
        2_000_000_000,
    )
    peer = moved(total, [(i, i ^ 8) for i in range(32)])
    own, send = call(
        response_kernel,
        [shaped((8, 64, 384), F32), shaped((8, 64, 384), F32)],
        [q, rows, scale, wu, prefix],
        2_000_000_000,
    )
    peer, own, send = lax.optimization_barrier((peer, own, send))
    other = lax.ppermute(send, "head", across)
    (joint,) = call(pass_kernel, [shaped((4, 128, 256), BF16)], [total, peer], 200_000_000)
    passed = moved(joint, [(z + 8 * x, z + 8 * (3 - x)) for x in (0, 1) for z in range(8)])
    (state,) = call(
        state_kernel, [shaped((4, 128, 256), BF16)], [peer, passed, before], 200_000_000
    )
    entered = lax.ppermute(state, "head", [(i + 1, i) for i in range(0, 8, 2)])
    keep, joined = call(
        output_kernel,
        [shaped((256, 512), BF16), shaped((256, 512), BF16)],
        [state, entered, own, other],
        500_000_000,
    )
    operands = [keep, joined, out_weight, other_weight]
    near = [(i, i ^ 2) for i in range(8)]
    far = [(i, i ^ 6) for i in range(8)]
    half = [shaped((128, CHUNK), BF16)] * 2
    routes = [near, near, far, far]
    sent = [None] * 4
    for part in range(2):
        to_near, to_far = call(
            functools.partial(send_kernel, part), half, operands, 500_000_000
        )
        operands[0], to_near, to_far = lax.optimization_barrier((operands[0], to_near, to_far))
        sent[part] = lax.ppermute(to_near, "head", near)
        sent[part + 2] = lax.ppermute(to_far, "head", far)
    final, passed = call(
        own_kernel, [shaped((64, 4096), BF16)] * 2, operands, 1_000_000_000
    )
    received = [None] * 4
    for part in (0, 2, 1, 3):
        (summed,) = call(
            functools.partial(pair_kernel, part),
            [shaped((64, CHUNK), BF16)],
            [passed, sent[part]],
            100_000,
        )
        received[part] = lax.ppermute(summed, "head", routes[3 - part])
    return call(sum_kernel, [shaped((64, 4096), BF16)], [final, *sent, *received], 1_000_000)[0]


def solution(mesh):
    return jax.shard_map(
        body,
        mesh=mesh,
        in_specs=(
            P("seq", "head", None),
            P("seq", "head", None),
            P("seq", "head", None),
            P("head", "seq"),
            P("seq", None),
            P("head", None),
        ),
        out_specs=P(("seq", "head"), None),
        check_vma=False,
    )
```

```python
import functools

import jax
import jax.numpy as jnp
from jax import lax
from jax.experimental import pallas as pl
from jax.experimental.pallas import tpu as pltpu
from jax.sharding import PartitionSpec as P

BLOCK = 128
INTERPRET = False
VMEM_LIMIT = 12 << 20
CHUNK = 1024
F32 = jnp.float32
BF16 = jnp.bfloat16


def split(x):
    high = x.astype(BF16)
    return high, (x - high.astype(F32)).astype(BF16)


def dot(a, b):
    return jnp.dot(a, b, preferred_element_type=F32)


def dot_t(a, b):
    return lax.dot_general(a, b, (((0,), (0,)), ((), ())), preferred_element_type=F32)


def dot_nt(a, b):
    return lax.dot_general(a, b, (((1,), (1,)), ((), ())), preferred_element_type=F32)


def dot3(a, b):
    a_high, a_low = split(a)
    b_high, b_low = split(b)
    left = jnp.concatenate([a_high, a_low], 1)
    right = jnp.concatenate([b_high, b_low], 1)
    both = dot(left, jnp.concatenate([right, right], 0))
    width = b.shape[1]
    return both[:, :width] + both[:, width:]


def dot2_right(a, b):
    b_high, b_low = split(b)
    return dot(jnp.concatenate([a, a], 1), jnp.concatenate([b_high, b_low], 0))


def dot2_left(a, b):
    a_high, a_low = split(a)
    return dot(jnp.concatenate([a_high, a_low], 1), jnp.concatenate([b, b], 0))


def square_ids(n):
    return lax.broadcasted_iota(jnp.int32, (n, n), 0), lax.broadcasted_iota(jnp.int32, (n, n), 1)


def head_rows(rows, width, place):
    row = lax.broadcasted_iota(jnp.int32, (BLOCK, width * BLOCK), 0)
    col = lax.broadcasted_iota(jnp.int32, (BLOCK, width * BLOCK), 1)
    chosen = jnp.where(col == width * row + place, 1.0, 0.0).astype(BF16)
    return dot(chosen, rows).astype(BF16)


CELLS = [(b, h) for b in range(4) for h in range(2)]


def after_map(first, second):
    added = jnp.concatenate([jnp.zeros((BLOCK, 128), F32), second[:, 128:]], 1)
    return dot3(second[:, :128], first) + added


def terms_kernel(resets_hbm, beta_hbm, k_hbm, v_ref, *refs):
    wu_ref, prefix_ref, scale_ref, rows_ref, carry_ref = refs[:5]
    resets, beta_ref, k_ref, sems = refs[5:]
    k_copy = pltpu.make_async_copy(k_hbm, k_ref, sems.at[2])
    resets_copy = pltpu.make_async_copy(resets_hbm, resets, sems.at[0])
    beta_copy = pltpu.make_async_copy(beta_hbm, beta_ref, sems.at[1])
    k_copy.start()
    beta_copy.start()
    resets_copy.start()
    row, col = square_ids(BLOCK)
    eye = row == col
    identity = jnp.where(eye, 1.0, 0.0).astype(F32)
    ks, vs, grams = {}, {}, {}
    k_copy.wait()
    for b, h in CELLS:
        ks[b, h] = head_rows(k_ref[b * 2 * BLOCK : (b + 1) * 2 * BLOCK], 2, h)
        vs[b, h] = v_ref[b * BLOCK : (b + 1) * BLOCK, h * 256 : (h + 1) * 256]
        rows_ref[b * 2 + h] = ks[b, h]
    for cell in CELLS:
        grams[cell] = dot_nt(ks[cell], ks[cell])
    beta_copy.wait()
    lower, inv, r_cols, beta_rows, c_rows = {}, {}, {}, {}, {}
    for b, h in CELLS:
        gram = grams[b, h]
        diagonal = jnp.where(eye, gram, 0.0)
        r_col = lax.rsqrt(jnp.sum(diagonal, axis=1, keepdims=True) + 1e-06)
        r_row = lax.rsqrt(jnp.sum(diagonal, axis=0, keepdims=True) + 1e-06)
        beta_row = beta_ref[h : h + 1, b * BLOCK : (b + 1) * BLOCK]
        beta_col = jnp.sum(jnp.where(eye, beta_row, 0.0), axis=1, keepdims=True)
        low = jnp.where(row > col, (beta_col * r_col) * gram * r_row, 0.0)
        lower[b, h] = low
        inv[b, h] = identity - jnp.where(row // 2 == col // 2, low, 0.0)
        r_cols[b, h] = r_col
        beta_rows[b, h] = beta_row
        c_rows[b, h] = beta_row * r_row
        scale_ref[b * 2 + h : b * 2 + h + 1, :] = r_row
    size = 2
    while size < BLOCK:
        joined = (row // (4 * size) == col // (4 * size)) & (row // size != col // size)
        links, squares, odds = {}, {}, {}
        for cell in CELLS:
            links[cell] = dot3(inv[cell], jnp.where(joined, lower[cell], 0.0))
        for cell in CELLS:
            squares[cell] = dot3(links[cell], links[cell])
            odds[cell] = inv[cell] - dot3(links[cell], inv[cell])
        for cell in CELLS:
            inv[cell] = odds[cell] + dot3(squares[cell], odds[cell])
        size *= 4
    resets_copy.wait()
    maps = {}
    kept = []
    for b in range(4):
        starts = (resets[0, 0] == b) | (resets[0, 1] == b)
        kept.append(jnp.where(starts, 0.0, 1.0).astype(F32))
    for b, h in CELLS:
        cell = (b, h)
        decay = dot2_left(inv[cell] * c_rows[cell], ks[cell])
        update = dot2_left(inv[cell] * beta_rows[cell], vs[cell])
        wu = jnp.concatenate([decay, update], 1)
        wu_ref[b * 2 + h] = wu
        high, low = split(wu * r_cols[cell])
        step = dot_t(jnp.concatenate([ks[cell], ks[cell]], 0), jnp.concatenate([high, low], 0))
        maps[cell] = jnp.concatenate([(identity - step[:, :128]) * kept[b], step[:, 128:]], 1)
    zeros = jnp.zeros((BLOCK, 256), F32)
    for h in range(2):
        first = after_map(maps[0, h], maps[1, h])
        last = after_map(maps[2, h], maps[3, h])
        whole = after_map(first, last)
        carry_ref[h] = jnp.concatenate(
            [whole[:, :128] - identity, whole[:, 128:]], 1
        ).astype(BF16)
        prefix_ref[h] = jnp.concatenate([identity, zeros], 1) * kept[0]
        prefix_ref[2 + h] = maps[0, h] * kept[1]
        prefix_ref[4 + h] = first * kept[2]
        prefix_ref[6 + h] = after_map(first, maps[2, h]) * kept[3]


def response_kernel(q_ref, k_ref, scale_ref, wu_ref, prefix_ref, r_ref, o_ref):
    row, col = square_ids(BLOCK)
    causal = row >= col
    for b, h in CELLS:
        cell = b * 2 + h
        q = head_rows(q_ref[b * 2 * BLOCK : (b + 1) * 2 * BLOCK], 2, h)
        qf = q.astype(F32)
        rq = lax.rsqrt(jnp.sum(qf * qf, axis=1, keepdims=True) + 1e-06)
        scores = rq * dot_nt(q, k_ref[cell]) * scale_ref[cell : cell + 1, :]
        local = dot3(jnp.where(causal, scores, 0.0), wu_ref[cell])
        reach = qf * rq - local[:, :128]
        out = dot3(reach, prefix_ref[cell])
        r_ref[cell] = out[:, :128].astype(BF16)
        o_ref[cell] = out[:, 128:] + local[:, 128:]


def follow(state, element):
    moved = dot2_right(element[:, :128], state)
    width = state.shape[1]
    added = element.astype(F32)
    if width == 256:
        added = added[:, 128:]
    else:
        added = jnp.concatenate([jnp.zeros((BLOCK, 128), F32), added[:, 128:]], 1)
    return state + moved + added


def whole_map(element, identity):
    element = element.astype(F32)
    return jnp.concatenate([element[:, :128] + identity, element[:, 128:]], 1)


def pair_map_kernel(own_ref, peer_ref, out_ref):
    row, col = square_ids(BLOCK)
    identity = jnp.where(row == col, 1.0, 0.0).astype(F32)
    upper = lax.axis_index("seq") % 2 == 1
    for h in range(2):
        early = jnp.where(upper, peer_ref[h], own_ref[h])
        late = jnp.where(upper, own_ref[h], peer_ref[h])
        both = follow(whole_map(early, identity), late)
        out_ref[h] = jnp.concatenate([both[:, :128] - identity, both[:, 128:]], 1).astype(BF16)


def group_kernel(peer_ref, pair_ref, first_ref, second_ref, far_ref, before_ref, total_ref):
    row, col = square_ids(BLOCK)
    identity = jnp.where(row == col, 1.0, 0.0).astype(F32)
    empty = jnp.concatenate([identity, jnp.zeros((BLOCK, 256), F32)], 1)
    z = lax.axis_index("seq") % 8
    place, upper = z // 2, z % 2 == 1
    for h in range(2):
        below = jnp.where(upper, second_ref[h], first_ref[h])
        above = jnp.where(upper, first_ref[h], second_ref[h])
        state = after = empty
        for step, element in ((1, above), (2, far_ref[h]), (3, below)):
            wraps = place + step == 4
            if step > 1:
                after = jnp.where(wraps, state, after)
                state = jnp.where(wraps, empty, state)
            state = follow(state, element)
        after = jnp.where(place == 0, state, after)
        state = jnp.where(place == 0, empty, state)
        before = jnp.where(upper, follow(state, peer_ref[h]), state)
        before_ref[h] = jnp.concatenate([before[:, :128] - identity, before[:, 128:]], 1)
        through = follow(state, pair_ref[h])
        total = dot3(after[:, :128], through)
        total_ref[h] = jnp.concatenate(
            [total[:, :128] - identity, total[:, 128:] + after[:, 128:]], 1
        ).astype(BF16)


def pass_kernel(own_ref, peer_ref, out_ref):
    odd = (lax.axis_index("seq") // 8) % 2 == 1
    for h in range(2):
        early = jnp.where(odd, peer_ref[h], own_ref[h])
        late = jnp.where(odd, own_ref[h], peer_ref[h])
        out_ref[h] = follow(early[:, 128:].astype(F32), late).astype(BF16)


def output_kernel(peer_ref, passed_ref, before_ref, r_ref, o_ref, keep_ref, send_ref):
    head = lax.axis_index("head")
    y, core = head // 2, head % 2
    odd = (lax.axis_index("seq") // 8) % 2 == 1
    states = []
    for h in range(2):
        state = passed_ref[h].astype(F32)
        state = jnp.where(odd, follow(state, peer_ref[h]), state)
        before = before_ref[h]
        states.append(state + dot3(before[:, :128], state) + before[:, 128:])
    for b in range(4):
        parts = []
        for h in range(2):
            cell = b * 2 + h
            out = dot2_right(r_ref[cell], states[h]) + o_ref[cell]
            mean = jnp.mean(out * out, axis=1, keepdims=True)
            parts.append((out * lax.rsqrt(mean + 1e-05)).astype(BF16))
        normed = jnp.concatenate(parts, 1)
        first, second = normed[:64], normed[64:]
        slot = pl.multiple_of(((4 - (y ^ b)) & 3) * 64, 64)
        keep_ref[pl.ds(slot, 64), :] = jnp.where(core == 0, first, second)
        send_ref[pl.ds(slot, 64), :] = jnp.where(core == 0, second, first)


HBM = pl.BlockSpec(memory_space=pltpu.HBM)
VMEM = pl.BlockSpec(memory_space=pltpu.VMEM)


def call(kernel, outs, arrays, flops, in_hbm=(), scratch=()):
    moved = sum(a.size * a.dtype.itemsize for a in (*in_hbm, *arrays, *outs))
    return pl.pallas_call(
        kernel,
        out_shape=[jax.ShapeDtypeStruct(a.shape, a.dtype) for a in outs],
        in_specs=[HBM] * len(in_hbm) + [VMEM] * len(arrays),
        out_specs=[VMEM] * len(outs),
        scratch_shapes=scratch,
        compiler_params=pltpu.CompilerParams(vmem_limit_bytes=VMEM_LIMIT),
        cost_estimate=pl.CostEstimate(flops=flops, bytes_accessed=moved, transcendentals=0),
        interpret=INTERPRET,
    )(*[pltpu.with_memory_space_constraint(a, pltpu.HBM) for a in in_hbm], *arrays)


def rows_product(own_rows, other_rows, own_w_ref, other_w_ref, first):
    columns = slice(first, first + CHUNK)
    out = dot(own_rows, own_w_ref[:, columns]) + dot(other_rows, other_w_ref[:, columns])
    return out.astype(BF16)


def send_kernel(part, keep_ref, joined_ref, own_w_ref, other_w_ref, near_ref, far_ref):
    weights = own_w_ref, other_w_ref, part * CHUNK
    near_ref[...] = rows_product(keep_ref[128:], joined_ref[128:], *weights)
    weights = own_w_ref, other_w_ref, 2048 + part * CHUNK
    far_ref[...] = rows_product(keep_ref[64:192], joined_ref[64:192], *weights)


def own_kernel(keep_ref, joined_ref, own_w_ref, other_w_ref, final_ref, passed_ref):
    for part in range(4):
        columns = slice(part * CHUNK, (part + 1) * CHUNK)
        weights = own_w_ref, other_w_ref, part * CHUNK
        if part < 2:
            out = rows_product(keep_ref[:128], joined_ref[:128], *weights)
        else:
            own_rows = jnp.concatenate([keep_ref[:64], keep_ref[192:]], 0)
            other_rows = jnp.concatenate([joined_ref[:64], joined_ref[192:]], 0)
            out = rows_product(own_rows, other_rows, *weights)
        final_ref[:, columns] = out[:64]
        passed_ref[:, columns] = out[64:]


def pair_kernel(part, passed_ref, sent_ref, out_ref):
    half = slice(0, 64) if part < 2 else slice(64, 128)
    own = passed_ref[:, part * CHUNK : (part + 1) * CHUNK].astype(F32)
    out_ref[...] = (own + sent_ref[half].astype(F32)).astype(BF16)


def sum_kernel(*refs):
    final_ref, out_ref = refs[0], refs[9]
    for part in range(4):
        columns = slice(part * CHUNK, (part + 1) * CHUNK)
        half = slice(64, 128) if part < 2 else slice(0, 64)
        total = final_ref[:, columns].astype(F32) + refs[1 + part][half].astype(F32)
        out_ref[:, columns] = (total + refs[5 + part][...].astype(F32)).astype(BF16)


def body(queries, keys, values, beta, reset_blocks, out_weight):
    q = queries.reshape(1024, 128)
    k = keys.reshape(1024, 128)
    v = values.reshape(512, 512)

    across = [(i, i ^ 1) for i in range(8)]
    other_weight = lax.ppermute(out_weight, "head", across)

    shaped = jax.ShapeDtypeStruct
    wu, prefix, scale, rows, carry = call(
        terms_kernel,
        [
            shaped((8, 128, 384), F32),
            shaped((8, 128, 384), F32),
            shaped((8, 128), F32),
            shaped((8, 128, 128), BF16),
            shaped((2, 128, 384), BF16),
        ],
        [v],
        3_000_000_000,
        in_hbm=[reset_blocks, beta, k],
        scratch=[
            pltpu.SMEM((1, 2), jnp.int32),
            pltpu.VMEM((2, 512), F32),
            pltpu.VMEM((1024, 128), BF16),
            pltpu.SemaphoreType.DMA((3,)),
        ],
    )
    inside = [(i, i ^ 1) for i in range(32)]
    outward = [(i, i - i % 8 + (i % 8 + (1 if i % 2 else 7)) % 8) for i in range(32)]
    neighbour = lax.ppermute(carry, "seq", inside)
    (pair,) = call(
        pair_map_kernel, [shaped((2, 128, 384), BF16)], [carry, neighbour], 100_000_000
    )
    first = lax.ppermute(pair, "seq", outward)
    second = lax.ppermute(first, "seq", inside)
    farthest = lax.ppermute(second, "seq", outward)
    before, total = call(
        group_kernel,
        [shaped((2, 128, 384), F32), shaped((2, 128, 384), BF16)],
        [neighbour, pair, first, second, farthest],
        600_000_000,
    )
    peer = lax.ppermute(total, "seq", [(i, i ^ 8) for i in range(32)])
    response, own_out = call(
        response_kernel,
        [shaped((8, 128, 128), BF16), shaped((8, 128, 256), F32)],
        [q, rows, scale, wu, prefix],
        2_000_000_000,
    )
    peer, response, own_out = lax.optimization_barrier((peer, response, own_out))
    (joint,) = call(pass_kernel, [shaped((2, 128, 256), BF16)], [total, peer], 100_000_000)
    passed = lax.ppermute(
        joint, "seq", [(z + 8 * x, z + 8 * (3 - x)) for x in (0, 1) for z in range(8)]
    )
    keep, send = call(
        output_kernel,
        [shaped((256, 512), BF16), shaped((256, 512), BF16)],
        [peer, passed, before, response, own_out],
        500_000_000,
    )
    joined = lax.ppermute(send, "head", across)
    operands = [keep, joined, out_weight, other_weight]
    near = [(i, i ^ 2) for i in range(8)]
    far = [(i, i ^ 6) for i in range(8)]
    half = [shaped((128, CHUNK), BF16)] * 2
    routes = [near, near, far, far]
    sent = [None] * 4
    for part in range(2):
        to_near, to_far = call(
            functools.partial(send_kernel, part), half, operands, 500_000_000
        )
        operands[0], to_near, to_far = lax.optimization_barrier((operands[0], to_near, to_far))
        sent[part] = lax.ppermute(to_near, "head", near)
        sent[part + 2] = lax.ppermute(to_far, "head", far)
    final, passed = call(
        own_kernel, [shaped((64, 4096), BF16)] * 2, operands, 1_000_000_000
    )
    received = [None] * 4
    for part in (0, 2, 1, 3):
        (summed,) = call(
            functools.partial(pair_kernel, part),
            [shaped((64, CHUNK), BF16)],
            [passed, sent[part]],
            100_000,
        )
        received[part] = lax.ppermute(summed, "head", routes[3 - part])
    return call(sum_kernel, [shaped((64, 4096), BF16)], [final, *sent, *received], 1_000_000)[0]


def solution(mesh):
    return jax.shard_map(
        body,
        mesh=mesh,
        in_specs=(
            P("seq", "head", None),
            P("seq", "head", None),
            P("seq", "head", None),
            P("head", "seq"),
            P("seq", None),
            P("head", None),
        ),
        out_specs=P(("seq", "head"), None),
        check_vma=False,
    )
```

```python
import functools

import jax
import jax.numpy as jnp
from jax import lax
from jax.experimental import pallas as pl
from jax.experimental.pallas import tpu as pltpu
from jax.sharding import PartitionSpec as P

BLOCK = 128
INTERPRET = False
VMEM_LIMIT = 12 << 20
CHUNK = 1024
F32 = jnp.float32
BF16 = jnp.bfloat16


def split(x):
    high = x.astype(BF16)
    return high, (x - high.astype(F32)).astype(BF16)


def dot(a, b):
    return jnp.dot(a, b, preferred_element_type=F32)


def dot_t(a, b):
    return lax.dot_general(a, b, (((0,), (0,)), ((), ())), preferred_element_type=F32)


def dot_nt(a, b):
    return lax.dot_general(a, b, (((1,), (1,)), ((), ())), preferred_element_type=F32)


def dot3(a, b):
    a_high, a_low = split(a)
    b_high, b_low = split(b)
    left = jnp.concatenate([a_high, a_low], 1)
    right = jnp.concatenate([b_high, b_low], 1)
    both = dot(left, jnp.concatenate([right, right], 0))
    width = b.shape[1]
    return both[:, :width] + both[:, width:]


def dot2_right(a, b):
    b_high, b_low = split(b)
    return dot(jnp.concatenate([a, a], 1), jnp.concatenate([b_high, b_low], 0))


def dot2_left(a, b):
    a_high, a_low = split(a)
    return dot(jnp.concatenate([a_high, a_low], 1), jnp.concatenate([b, b], 0))


def square_ids(n):
    return lax.broadcasted_iota(jnp.int32, (n, n), 0), lax.broadcasted_iota(jnp.int32, (n, n), 1)


def head_rows(rows, width, place):
    row = lax.broadcasted_iota(jnp.int32, (BLOCK, width * BLOCK), 0)
    col = lax.broadcasted_iota(jnp.int32, (BLOCK, width * BLOCK), 1)
    chosen = jnp.where(col == width * row + place, 1.0, 0.0).astype(BF16)
    return dot(chosen, rows).astype(BF16)


CELLS = [(b, h) for b in range(4) for h in range(2)]


def after_map(first, second):
    added = jnp.concatenate([jnp.zeros((BLOCK, 128), F32), second[:, 128:]], 1)
    return dot3(second[:, :128], first) + added


def terms_kernel(resets_hbm, beta_hbm, k_hbm, v_ref, *refs):
    wu_ref, prefix_ref, scale_ref, rows_ref = refs[:4]
    carry_refs = refs[4:6]
    resets, beta_ref, k_ref, sems = refs[6:]
    k_copy = pltpu.make_async_copy(k_hbm, k_ref, sems.at[2])
    resets_copy = pltpu.make_async_copy(resets_hbm, resets, sems.at[0])
    beta_copy = pltpu.make_async_copy(beta_hbm, beta_ref, sems.at[1])
    k_copy.start()
    beta_copy.start()
    resets_copy.start()
    row, col = square_ids(BLOCK)
    eye = row == col
    identity = jnp.where(eye, 1.0, 0.0).astype(F32)
    ks, vs, grams = {}, {}, {}
    k_copy.wait()
    for b, h in CELLS:
        ks[b, h] = head_rows(k_ref[b * 2 * BLOCK : (b + 1) * 2 * BLOCK], 2, h)
        vs[b, h] = v_ref[b * BLOCK : (b + 1) * BLOCK, h * 256 : (h + 1) * 256]
        rows_ref[b * 2 + h] = ks[b, h]
    for cell in CELLS:
        grams[cell] = dot_nt(ks[cell], ks[cell])
    beta_copy.wait()
    lower, inv, r_cols, beta_rows, c_rows = {}, {}, {}, {}, {}
    for b, h in CELLS:
        gram = grams[b, h]
        diagonal = jnp.where(eye, gram, 0.0)
        r_col = lax.rsqrt(jnp.sum(diagonal, axis=1, keepdims=True) + 1e-06)
        r_row = lax.rsqrt(jnp.sum(diagonal, axis=0, keepdims=True) + 1e-06)
        beta_row = beta_ref[h : h + 1, b * BLOCK : (b + 1) * BLOCK]
        beta_col = jnp.sum(jnp.where(eye, beta_row, 0.0), axis=1, keepdims=True)
        low = jnp.where(row > col, (beta_col * r_col) * gram * r_row, 0.0)
        lower[b, h] = low
        inv[b, h] = identity - jnp.where(row // 2 == col // 2, low, 0.0)
        r_cols[b, h] = r_col
        beta_rows[b, h] = beta_row
        c_rows[b, h] = beta_row * r_row
        scale_ref[b * 2 + h : b * 2 + h + 1, :] = r_row
    size = 2
    while size < BLOCK:
        joined = (row // (4 * size) == col // (4 * size)) & (row // size != col // size)
        links, squares, odds = {}, {}, {}
        for cell in CELLS:
            links[cell] = dot3(inv[cell], jnp.where(joined, lower[cell], 0.0))
        for cell in CELLS:
            squares[cell] = dot3(links[cell], links[cell])
            odds[cell] = inv[cell] - dot3(links[cell], inv[cell])
        for cell in CELLS:
            inv[cell] = odds[cell] + dot3(squares[cell], odds[cell])
        size *= 4
    resets_copy.wait()
    maps = {}
    kept = []
    for b in range(4):
        starts = (resets[0, 0] == b) | (resets[0, 1] == b)
        kept.append(jnp.where(starts, 0.0, 1.0).astype(F32))
    for b, h in CELLS:
        cell = (b, h)
        decay = dot2_left(inv[cell] * c_rows[cell], ks[cell])
        update = dot2_left(inv[cell] * beta_rows[cell], vs[cell])
        wu = jnp.concatenate([decay, update], 1)
        wu_ref[b * 2 + h] = wu
        high, low = split(wu * r_cols[cell])
        step = dot_t(jnp.concatenate([ks[cell], ks[cell]], 0), jnp.concatenate([high, low], 0))
        maps[cell] = jnp.concatenate([(identity - step[:, :128]) * kept[b], step[:, 128:]], 1)
    zeros = jnp.zeros((BLOCK, 256), F32)
    for h in range(2):
        first = after_map(maps[0, h], maps[1, h])
        last = after_map(maps[2, h], maps[3, h])
        whole = after_map(first, last)
        carry_refs[h][...] = jnp.concatenate(
            [whole[:, :128] - identity, whole[:, 128:]], 1
        ).astype(BF16)
        prefix_ref[h] = jnp.concatenate([identity, zeros], 1) * kept[0]
        prefix_ref[2 + h] = maps[0, h] * kept[1]
        prefix_ref[4 + h] = first * kept[2]
        prefix_ref[6 + h] = after_map(first, maps[2, h]) * kept[3]


def response_kernel(q_ref, k_ref, scale_ref, wu_ref, prefix_ref, r_ref, o_ref):
    row, col = square_ids(BLOCK)
    causal = row >= col
    for b, h in CELLS:
        cell = b * 2 + h
        q = head_rows(q_ref[b * 2 * BLOCK : (b + 1) * 2 * BLOCK], 2, h)
        qf = q.astype(F32)
        rq = lax.rsqrt(jnp.sum(qf * qf, axis=1, keepdims=True) + 1e-06)
        scores = rq * dot_nt(q, k_ref[cell]) * scale_ref[cell : cell + 1, :]
        local = dot3(jnp.where(causal, scores, 0.0), wu_ref[cell])
        reach = qf * rq - local[:, :128]
        out = dot3(reach, prefix_ref[cell])
        r_ref[cell] = out[:, :128].astype(BF16)
        o_ref[cell] = out[:, 128:] + local[:, 128:]


def follow(state, element):
    moved = dot2_right(element[:, :128], state)
    width = state.shape[1]
    added = element.astype(F32)
    if width == 256:
        added = added[:, 128:]
    else:
        added = jnp.concatenate([jnp.zeros((BLOCK, 128), F32), added[:, 128:]], 1)
    return state + moved + added


def whole_map(element, identity):
    element = element.astype(F32)
    return jnp.concatenate([element[:, :128] + identity, element[:, 128:]], 1)


def pair_map_kernel(own_ref, peer_ref, out_ref):
    row, col = square_ids(BLOCK)
    identity = jnp.where(row == col, 1.0, 0.0).astype(F32)
    upper = lax.axis_index("seq") % 2 == 1
    early = jnp.where(upper, peer_ref[...], own_ref[...])
    late = jnp.where(upper, own_ref[...], peer_ref[...])
    both = follow(whole_map(early, identity), late)
    out_ref[...] = jnp.concatenate([both[:, :128] - identity, both[:, 128:]], 1).astype(BF16)


def group_kernel(*refs):
    before_ref, total_ref = refs[10:]
    row, col = square_ids(BLOCK)
    identity = jnp.where(row == col, 1.0, 0.0).astype(F32)
    empty = jnp.concatenate([identity, jnp.zeros((BLOCK, 256), F32)], 1)
    z = lax.axis_index("seq") % 8
    place, upper = z // 2, z % 2 == 1
    for h in range(2):
        peer, pair, first, second, far = (ref[...] for ref in refs[5 * h : 5 * h + 5])
        below = jnp.where(upper, second, first)
        above = jnp.where(upper, first, second)
        state = after = empty
        for step, element in ((1, above), (2, far), (3, below)):
            wraps = place + step == 4
            if step > 1:
                after = jnp.where(wraps, state, after)
                state = jnp.where(wraps, empty, state)
            state = follow(state, element)
        after = jnp.where(place == 0, state, after)
        state = jnp.where(place == 0, empty, state)
        before = jnp.where(upper, follow(state, peer), state)
        before_ref[h] = jnp.concatenate([before[:, :128] - identity, before[:, 128:]], 1)
        through = follow(state, pair)
        total = dot3(after[:, :128], through)
        total_ref[h] = jnp.concatenate(
            [total[:, :128] - identity, total[:, 128:] + after[:, 128:]], 1
        ).astype(BF16)


def pass_kernel(own_ref, peer_ref, out_ref):
    odd = (lax.axis_index("seq") // 8) % 2 == 1
    for h in range(2):
        early = jnp.where(odd, peer_ref[h], own_ref[h])
        late = jnp.where(odd, own_ref[h], peer_ref[h])
        out_ref[h] = follow(early[:, 128:].astype(F32), late).astype(BF16)


def output_kernel(peer_ref, passed_ref, before_ref, r_ref, o_ref, keep_ref, send_ref):
    head = lax.axis_index("head")
    y, core = head // 2, head % 2
    odd = (lax.axis_index("seq") // 8) % 2 == 1
    states = []
    for h in range(2):
        state = passed_ref[h].astype(F32)
        state = jnp.where(odd, follow(state, peer_ref[h]), state)
        before = before_ref[h]
        states.append(state + dot3(before[:, :128], state) + before[:, 128:])
    for b in range(4):
        parts = []
        for h in range(2):
            cell = b * 2 + h
            out = dot2_right(r_ref[cell], states[h]) + o_ref[cell]
            mean = jnp.mean(out * out, axis=1, keepdims=True)
            parts.append((out * lax.rsqrt(mean + 1e-05)).astype(BF16))
        normed = jnp.concatenate(parts, 1)
        first, second = normed[:64], normed[64:]
        slot = pl.multiple_of(((4 - (y ^ b)) & 3) * 64, 64)
        keep_ref[pl.ds(slot, 64), :] = jnp.where(core == 0, first, second)
        send_ref[pl.ds(slot, 64), :] = jnp.where(core == 0, second, first)


HBM = pl.BlockSpec(memory_space=pltpu.HBM)
VMEM = pl.BlockSpec(memory_space=pltpu.VMEM)


def call(kernel, outs, arrays, flops, in_hbm=(), scratch=()):
    moved = sum(a.size * a.dtype.itemsize for a in (*in_hbm, *arrays, *outs))
    return pl.pallas_call(
        kernel,
        out_shape=[jax.ShapeDtypeStruct(a.shape, a.dtype) for a in outs],
        in_specs=[HBM] * len(in_hbm) + [VMEM] * len(arrays),
        out_specs=[VMEM] * len(outs),
        scratch_shapes=scratch,
        compiler_params=pltpu.CompilerParams(vmem_limit_bytes=VMEM_LIMIT),
        cost_estimate=pl.CostEstimate(flops=flops, bytes_accessed=moved, transcendentals=0),
        interpret=INTERPRET,
    )(*[pltpu.with_memory_space_constraint(a, pltpu.HBM) for a in in_hbm], *arrays)


def rows_product(own_rows, other_rows, own_w_ref, other_w_ref, first):
    columns = slice(first, first + CHUNK)
    out = dot(own_rows, own_w_ref[:, columns]) + dot(other_rows, other_w_ref[:, columns])
    return out.astype(BF16)


def send_kernel(part, keep_ref, joined_ref, own_w_ref, other_w_ref, near_ref, far_ref):
    weights = own_w_ref, other_w_ref, part * CHUNK
    near_ref[...] = rows_product(keep_ref[128:], joined_ref[128:], *weights)
    weights = own_w_ref, other_w_ref, 2048 + part * CHUNK
    far_ref[...] = rows_product(keep_ref[64:192], joined_ref[64:192], *weights)


def own_kernel(keep_ref, joined_ref, own_w_ref, other_w_ref, final_ref, passed_ref):
    for part in range(4):
        columns = slice(part * CHUNK, (part + 1) * CHUNK)
        weights = own_w_ref, other_w_ref, part * CHUNK
        if part < 2:
            out = rows_product(keep_ref[:128], joined_ref[:128], *weights)
        else:
            own_rows = jnp.concatenate([keep_ref[:64], keep_ref[192:]], 0)
            other_rows = jnp.concatenate([joined_ref[:64], joined_ref[192:]], 0)
            out = rows_product(own_rows, other_rows, *weights)
        final_ref[:, columns] = out[:64]
        passed_ref[:, columns] = out[64:]


def pair_kernel(part, passed_ref, sent_ref, out_ref):
    half = slice(0, 64) if part < 2 else slice(64, 128)
    own = passed_ref[:, part * CHUNK : (part + 1) * CHUNK].astype(F32)
    out_ref[...] = (own + sent_ref[half].astype(F32)).astype(BF16)


def sum_kernel(*refs):
    final_ref, out_ref = refs[0], refs[9]
    for part in range(4):
        columns = slice(part * CHUNK, (part + 1) * CHUNK)
        half = slice(64, 128) if part < 2 else slice(0, 64)
        total = final_ref[:, columns].astype(F32) + refs[1 + part][half].astype(F32)
        out_ref[:, columns] = (total + refs[5 + part][...].astype(F32)).astype(BF16)


def body(queries, keys, values, beta, reset_blocks, out_weight):
    q = queries.reshape(1024, 128)
    k = keys.reshape(1024, 128)
    v = values.reshape(512, 512)

    across = [(i, i ^ 1) for i in range(8)]
    other_weight = lax.ppermute(out_weight, "head", across)

    shaped = jax.ShapeDtypeStruct
    wu, prefix, scale, rows, *carries = call(
        terms_kernel,
        [
            shaped((8, 128, 384), F32),
            shaped((8, 128, 384), F32),
            shaped((8, 128), F32),
            shaped((8, 128, 128), BF16),
            shaped((128, 384), BF16),
            shaped((128, 384), BF16),
        ],
        [v],
        3_000_000_000,
        in_hbm=[reset_blocks, beta, k],
        scratch=[
            pltpu.SMEM((1, 2), jnp.int32),
            pltpu.VMEM((2, 512), F32),
            pltpu.VMEM((1024, 128), BF16),
            pltpu.SemaphoreType.DMA((3,)),
        ],
    )
    inside = [(i, i ^ 1) for i in range(32)]
    outward = [(i, i - i % 8 + (i % 8 + (1 if i % 2 else 7)) % 8) for i in range(32)]
    gathered = []
    for carry in carries:
        neighbour = lax.ppermute(carry, "seq", inside)
        (pair,) = call(
            pair_map_kernel, [shaped((128, 384), BF16)], [carry, neighbour], 100_000_000
        )
        first = lax.ppermute(pair, "seq", outward)
        second = lax.ppermute(first, "seq", inside)
        farthest = lax.ppermute(second, "seq", outward)
        gathered += [neighbour, pair, first, second, farthest]
    before, total = call(
        group_kernel,
        [shaped((2, 128, 384), F32), shaped((2, 128, 384), BF16)],
        gathered,
        600_000_000,
    )
    peer = lax.ppermute(total, "seq", [(i, i ^ 8) for i in range(32)])
    response, own_out = call(
        response_kernel,
        [shaped((8, 128, 128), BF16), shaped((8, 128, 256), F32)],
        [q, rows, scale, wu, prefix],
        2_000_000_000,
    )
    peer, response, own_out = lax.optimization_barrier((peer, response, own_out))
    (joint,) = call(pass_kernel, [shaped((2, 128, 256), BF16)], [total, peer], 100_000_000)
    passed = lax.ppermute(
        joint, "seq", [(z + 8 * x, z + 8 * (3 - x)) for x in (0, 1) for z in range(8)]
    )
    keep, send = call(
        output_kernel,
        [shaped((256, 512), BF16), shaped((256, 512), BF16)],
        [peer, passed, before, response, own_out],
        500_000_000,
    )
    joined = lax.ppermute(send, "head", across)
    operands = [keep, joined, out_weight, other_weight]
    near = [(i, i ^ 2) for i in range(8)]
    far = [(i, i ^ 6) for i in range(8)]
    half = [shaped((128, CHUNK), BF16)] * 2
    routes = [near, near, far, far]
    sent = [None] * 4
    for part in range(2):
        to_near, to_far = call(
            functools.partial(send_kernel, part), half, operands, 500_000_000
        )
        operands[0], to_near, to_far = lax.optimization_barrier((operands[0], to_near, to_far))
        sent[part] = lax.ppermute(to_near, "head", near)
        sent[part + 2] = lax.ppermute(to_far, "head", far)
    final, passed = call(
        own_kernel, [shaped((64, 4096), BF16)] * 2, operands, 1_000_000_000
    )
    received = [None] * 4
    for part in (0, 2, 1, 3):
        (summed,) = call(
            functools.partial(pair_kernel, part),
            [shaped((64, CHUNK), BF16)],
            [passed, sent[part]],
            100_000,
        )
        received[part] = lax.ppermute(summed, "head", routes[3 - part])
    return call(sum_kernel, [shaped((64, 4096), BF16)], [final, *sent, *received], 1_000_000)[0]


def solution(mesh):
    return jax.shard_map(
        body,
        mesh=mesh,
        in_specs=(
            P("seq", "head", None),
            P("seq", "head", None),
            P("seq", "head", None),
            P("head", "seq"),
            P("seq", None),
            P("head", None),
        ),
        out_specs=P(("seq", "head"), None),
        check_vma=False,
    )
```
